512 devices in a mesh: seq: 16 (over y_hi, z), head: 32 (over x, y_lo, core).
Axes of the slice: x: 4, y: 8 (y_hi: 2, y_lo: 4; y = y_hi * 4 + y_lo), z: 8, core: 2. Of those that a mesh axis runs over, the one named last changes fastest.
Arguments:
- tokens: bfloat16 [16384, 4096], P(('seq', 'head')), may hold values from -6 to 6
- doc_lengths: int32 [16], replicated, may hold values from 1 to 8704, as said below
- value_weight: bfloat16 [4096, 8192], P('seq', 'head'), may hold values from -0.09375 to 0.09375
- gate_weight: bfloat16 [4096, 8192], P('seq', 'head'), may hold values from -0.09375 to 0.09375
- state_weight: bfloat16 [8, 4096, 256], P(None, 'seq'), may hold values from -0.09375 to 0.09375
- step_weight: bfloat16 [4096, 128], P('seq', 'head'), may hold values from -0.09375 to 0.09375
- value_conv: float32 [4, 8192], P(None, 'head'), may hold values from -3 to 3
- state_conv: float32 [8, 4, 256], replicated, may hold values from -3 to 3
- step_bias: float32 [128], P('head'), may hold values from -5 to -3
- log_rate: float32 [128], P('head'), may hold values from -6 to 4
Outputs:
- layer_output: bfloat16 [16384, 8192], P('seq', 'head')
The draws below stay inside these ranges and needn't reach their ends.
Inputs may be any that keep to these rules, and one draw needn't show every extreme that they name: `doc_lengths`: the 16 documents lie one after another, their lengths sum to 16384, and the last one holds 8704 positions.
All inputs are finite; a program needn't handle non-finite values.
Results may differ from the reference program's by a relative error of at most 0.015.
Values may be sent and summed in bfloat16 or wider, within the bound.
No kernel may reach another device: no remote copies, remote signals or barrier semaphores. Data moves between devices by JAX's collectives and lax.ppermute only.
A program may use at most 64 MiB of HBM per device.

```python
import jax
import jax.numpy as jnp
from jax import lax

D = 4096
HEADS = 128
HEAD_DIM = 64
STATE = 128
GROUPS = 8
BLOCK = 256
CONV = 4
DOCS = 16
TOK_DEV = 1024
TOKENS = 16384


def draw_doc_lengths(key, part):
    longest = TOKENS // 2 + TOK_DEV // 2
    remaining = TOKENS - longest
    shuffled = jax.random.permutation(jax.random.fold_in(key, 17), remaining - 1)
    cut_points = jnp.sort(shuffled[:DOCS - 2] + 1).astype(jnp.int32)
    edges = jnp.concatenate([jnp.zeros((1,), jnp.int32), cut_points, jnp.full((1,), remaining, jnp.int32)])
    leading = (edges[1:] - edges[:-1]).astype(jnp.int32)
    return jnp.concatenate([leading, jnp.full((1,), longest, jnp.int32)]).astype(jnp.int32)


def block_levels(stream_key, shape, split, low, high):
    factor_of, own = 1.0, jax.random.fold_in(stream_key, 6)
    for dim, parts in split:
        steps = jnp.exp(jax.random.uniform(jax.random.fold_in(own, dim), (parts,), jnp.float32, low / len(split), high / len(split)))
        factor_of = factor_of * jnp.repeat(steps, shape[dim] // parts).reshape([-1 if axis == dim else 1 for axis in range(len(shape))])
    return factor_of


def noise(key, dims, scale, bound, cuts=(), held_as=jnp.bfloat16):
    array = scale * jax.random.normal(key, dims, jnp.float32)
    if cuts:
        array = array * block_levels(key, dims, cuts, -0.22, 0.18)
    return jnp.clip(array, -bound, bound).astype(held_as)


def setup_inputs(seed: int = 0) -> dict:
    splits = jax.random.split(jax.random.key(seed), 11)
    tokens = noise(splits[0], (TOKENS, D), 1.0, 6.0, ((0, 512),))
    doc_lengths = draw_doc_lengths(jax.random.fold_in(splits[10], 71), 0)
    value_weight = noise(splits[2], (D, HEADS * HEAD_DIM), D ** -0.5, 0.09375, ((0, 16), (1, 32)))
    gate_weight = noise(splits[3], (D, HEADS * HEAD_DIM), D ** -0.5, 0.09375, ((0, 16), (1, 32)))
    state_weight = noise(splits[4], (GROUPS, D, 2 * STATE), D ** -0.5, 0.09375, ((1, 16),))
    step_weight = noise(splits[5], (D, HEADS), D ** -0.5, 0.09375, ((0, 16), (1, 32)))
    value_conv = noise(splits[6], (CONV, HEADS * HEAD_DIM), CONV ** -0.5, 3.0, ((1, 32),), jnp.float32)
    state_conv = noise(splits[7], (GROUPS, CONV, 2 * STATE), CONV ** -0.5, 3.0, (), jnp.float32)
    step_bias = jnp.clip(-5.0 + 2.0 * jax.random.uniform(splits[8], (HEADS,), jnp.float32) ** block_levels(splits[8], (HEADS,), ((0, 32),), -0.2, 0.2), -5.0, -3.0)
    log_rate = jnp.clip(-6.0 + 10.0 * jax.random.uniform(splits[9], (HEADS,), jnp.float32) ** block_levels(splits[9], (HEADS,), ((0, 32),), -0.2, 0.2), -6.0, 4.0)
    return {"tokens": tokens, "doc_lengths": doc_lengths, "value_weight": value_weight, "gate_weight": gate_weight, "state_weight": state_weight, "step_weight": step_weight, "value_conv": value_conv, "state_conv": state_conv, "step_bias": step_bias, "log_rate": log_rate}


def segment_of(positions, starts):
    reached = (starts[None, :] <= positions[:, None]).astype(jnp.int32)
    return (jnp.sum(reached, axis=1) - 1).astype(jnp.int32)


def causal_conv(extended, taps_weight, seg_ext, row_count):
    tap_count = taps_weight.shape[0]
    own_segment = seg_ext[tap_count - 1:]
    summed = jnp.zeros((row_count, extended.shape[1]), jnp.float32)
    for tap_index in range(tap_count):
        window = extended[tap_index:tap_index + row_count].astype(jnp.float32)
        keep_mask = (seg_ext[tap_index:tap_index + row_count] == own_segment).astype(jnp.float32)[:, None]
        summed = summed + taps_weight[tap_index].astype(jnp.float32)[None, :] * window * keep_mask
    return jax.nn.silu(summed).astype(jnp.bfloat16)


def block_terms(b_rows, c_rows, x_rows, decay_rows, step_rows, segments, seg_before):
    block_len = b_rows.shape[0]
    head_total = decay_rows.shape[0]
    x_heads = x_rows.reshape(block_len, head_total, -1)
    cumulative = jnp.cumsum(decay_rows, axis=1)
    products = jnp.dot(c_rows, b_rows.T, preferred_element_type=jnp.float32)
    local_index = jnp.arange(block_len)
    allowed = (local_index[None, :] <= local_index[:, None]) & (segments[None, :] == segments[:, None])
    spread = cumulative[:, :, None] - cumulative[:, None, :]
    decay_mat = jnp.where(allowed[None], jnp.exp(jnp.where(allowed[None], spread, 0.0)), 0.0)
    scores = (products[None] * decay_mat * step_rows[:, None, :]).astype(jnp.bfloat16)
    y_inner = jnp.einsum("hij,jhp->ihp", scores, x_heads, preferred_element_type=jnp.float32)
    ending = cumulative[:, -1]
    trailing = jnp.where((segments == segments[-1])[None, :], jnp.exp(ending[:, None] - cumulative), 0.0) * step_rows
    weighted = (trailing.T[:, :, None] * x_heads.astype(jnp.float32)).astype(jnp.bfloat16)
    local_state = jnp.einsum("jn,jhp->hnp", b_rows, weighted, preferred_element_type=jnp.float32)
    factor = jnp.where(segments[-1] == seg_before, jnp.exp(ending), 0.0)
    entry_gain = jnp.where((segments == seg_before)[None, :], jnp.exp(cumulative), 0.0)
    return y_inner.reshape(block_len, -1), local_state, factor, entry_gain


def local_pass(state_cols, value_cols, decay_cols, step_cols, seg_rows, seg_before, block_len):
    block_count = state_cols.shape[0] // block_len
    state_dim = state_cols.shape[1] // 2
    head_total = decay_cols.shape[1]
    b_all = state_cols[:, :state_dim].reshape(block_count, block_len, state_dim)
    c_all = state_cols[:, state_dim:].reshape(block_count, block_len, state_dim)
    x_all = value_cols.reshape(block_count, block_len, -1)
    decay_all = decay_cols.reshape(block_count, block_len, head_total).transpose(0, 2, 1)
    step_all = step_cols.reshape(block_count, block_len, head_total).transpose(0, 2, 1)
    seg_all = seg_rows.reshape(block_count, block_len)

    def one_block(block_item):
        return block_terms(*block_item)

    outputs = lax.map(one_block, (b_all, c_all, x_all, decay_all, step_all, seg_all, seg_before))
    return outputs, c_all


def prefix_blocks(local_state, factor):
    def chain_step(carry_pair, block_item):
        running, running_gain = carry_pair
        local_term, factor_term = block_item
        return (factor_term[:, None, None] * running + local_term, factor_term * running_gain), (running, running_gain)

    initial = (jnp.zeros(local_state.shape[1:], jnp.float32), jnp.ones((factor.shape[1],), jnp.float32))
    (shard_state, shard_gain), (inside, gain_list) = lax.scan(chain_step, initial, (local_state, factor))
    return shard_state, shard_gain, inside, gain_list


def finish(y_inner, incoming, entry_gain, c_all, value_cols, gate_cols):
    block_count, block_len, _ = y_inner.shape
    head_total = incoming.shape[1]
    carried = jnp.einsum("cin,chnp->cihp", c_all.astype(jnp.float32), incoming, precision=lax.Precision.HIGHEST)
    carried = carried * entry_gain.transpose(0, 2, 1)[:, :, :, None]
    x_heads = value_cols.reshape(block_count, block_len, head_total, -1).astype(jnp.float32)
    summed = y_inner.reshape(block_count, block_len, head_total, -1) + carried + x_heads
    gating = jax.nn.silu(gate_cols.astype(jnp.float32)).reshape(block_count, block_len, head_total, -1)
    return (summed * gating).reshape(block_count * block_len, -1).astype(jnp.bfloat16)


def reference(tokens, doc_lengths, value_weight, gate_weight, state_weight, step_weight, value_conv, state_conv, step_bias, log_rate):
    tap_count = CONV
    starts = (jnp.cumsum(doc_lengths) - doc_lengths).astype(jnp.int32)
    positions = jnp.arange(-(tap_count - 1), TOKENS).astype(jnp.int32)
    seg_ext = segment_of(positions, starts)
    state_flat = state_weight.transpose(1, 0, 2).reshape(D, GROUPS * 2 * STATE)
    value_proj = jnp.dot(tokens, value_weight, preferred_element_type=jnp.float32).astype(jnp.bfloat16)
    gate_proj = jnp.dot(tokens, gate_weight, preferred_element_type=jnp.float32).astype(jnp.bfloat16)
    state_proj = jnp.dot(tokens, state_flat, preferred_element_type=jnp.float32).astype(jnp.bfloat16)
    step_proj = jnp.dot(tokens, step_weight, preferred_element_type=jnp.float32).astype(jnp.bfloat16)
    value_ext = jnp.concatenate([jnp.zeros((tap_count - 1, value_proj.shape[1]), jnp.bfloat16), value_proj], axis=0)
    state_ext = jnp.concatenate([jnp.zeros((tap_count - 1, state_proj.shape[1]), jnp.bfloat16), state_proj], axis=0)
    value_act = causal_conv(value_ext, value_conv, seg_ext, TOKENS)
    conv_flat = state_conv.transpose(1, 0, 2).reshape(tap_count, GROUPS * 2 * STATE)
    state_act = causal_conv(state_ext, conv_flat, seg_ext, TOKENS)
    step_size = jax.nn.softplus(step_proj.astype(jnp.float32) + step_bias[None, :])
    decay_rate = -jnp.exp(log_rate)[None, :] * step_size
    seg_rows = seg_ext[tap_count - 1:]
    seg_before = seg_ext[tap_count - 2:tap_count - 2 + TOKENS:BLOCK]
    per_group = HEADS // GROUPS

    def group_out(group_index):
        state_cols = lax.dynamic_slice_in_dim(state_act, group_index * 2 * STATE, 2 * STATE, 1)
        value_cols = lax.dynamic_slice_in_dim(value_act, group_index * per_group * HEAD_DIM, per_group * HEAD_DIM, 1)
        gate_cols = lax.dynamic_slice_in_dim(gate_proj, group_index * per_group * HEAD_DIM, per_group * HEAD_DIM, 1)
        decay_cols = lax.dynamic_slice_in_dim(decay_rate, group_index * per_group, per_group, 1)
        step_cols = lax.dynamic_slice_in_dim(step_size, group_index * per_group, per_group, 1)
        (y_inner, local_state, factor, entry_gain), c_all = local_pass(state_cols, value_cols, decay_cols, step_cols, seg_rows, seg_before, BLOCK)
        shard_state, shard_gain, inside, gain_list = prefix_blocks(local_state, factor)
        return finish(y_inner, inside, entry_gain, c_all, value_cols, gate_cols)

    blocks = lax.map(group_out, jnp.arange(GROUPS).astype(jnp.int32))
    return blocks.transpose(1, 0, 2).reshape(TOKENS, HEADS * HEAD_DIM)
```

```python
import jax
import jax.numpy as jnp
from jax import lax
from jax.sharding import Mesh
from jax.sharding import PartitionSpec as P

HEADS = 128
GROUPS = 8
BLOCK = 256
STATE = 128
YH, Z, X, Y, C = 2, 8, 4, 4, 2
SEQ = ("yh", "z")
HEAD = ("x", "y", "c")
F32 = jnp.float32
BF16 = jnp.bfloat16


def ring(count, step):
    return [(i, (i + step) % count) for i in range(count)]


def along_seq(value, step):
    return lax.ppermute(value, SEQ, [(i, i + step) for i in range(YH * Z - step)])


def ring_gather(block):
    half = block.shape[1] // 2
    right = left = block
    z = lax.axis_index("z")
    held = jnp.zeros((Z,) + block.shape, block.dtype)

    def put(held, piece, offset, row):
        return lax.dynamic_update_slice(held, piece[None], ((z + offset) % Z, 0, row, 0))

    held = put(held, block, 0, 0)
    for step in range(1, 4):
        right = lax.ppermute(right, "z", ring(Z, 1))
        left = lax.ppermute(left, "z", ring(Z, -1))
        held = put(held, right, -step + Z, 0)
        held = put(held, left, step, 0)
    right = lax.ppermute(right[:, :half], "z", ring(Z, 1))
    left = lax.ppermute(left[:, half:], "z", ring(Z, -1))
    held = put(held, right, 4, 0)
    held = put(held, left, 4, half)
    return held


def segment_of(positions, starts):
    reached = (starts[None, :] <= positions[:, None]).astype(jnp.int32)
    return jnp.sum(reached, axis=1) - 1


def causal_conv(extended, taps_weight, seg_ext, row_count):
    tap_count = taps_weight.shape[0]
    own_segment = seg_ext[tap_count - 1 :]
    summed = jnp.zeros((row_count, extended.shape[1]), F32)
    for tap_index in range(tap_count):
        window = extended[tap_index : tap_index + row_count].astype(F32)
        keep_mask = (seg_ext[tap_index : tap_index + row_count] == own_segment).astype(F32)
        summed = summed + taps_weight[tap_index][None, :] * window * keep_mask[:, None]
    return jax.nn.silu(summed).astype(BF16)


def block_terms(b_rows, c_rows, x_rows, decay_rows, step_rows, segments, seg_before):
    block_len = b_rows.shape[0]
    head_total = decay_rows.shape[0]
    x_heads = x_rows.reshape(block_len, head_total, -1)
    cumulative = jnp.cumsum(decay_rows, axis=1)
    products = jnp.dot(c_rows, b_rows.T, preferred_element_type=F32)
    local_index = jnp.arange(block_len)
    allowed = (local_index[None, :] <= local_index[:, None]) & (
        segments[None, :] == segments[:, None]
    )
    spread = cumulative[:, :, None] - cumulative[:, None, :]
    decay_mat = jnp.where(allowed[None], jnp.exp(jnp.where(allowed[None], spread, 0.0)), 0.0)
    scores = (products[None] * decay_mat * step_rows[:, None, :]).astype(BF16)
    y_inner = jnp.einsum("hij,jhp->ihp", scores, x_heads, preferred_element_type=F32)
    ending = cumulative[:, -1]
    trailing = (
        jnp.where((segments == segments[-1])[None, :], jnp.exp(ending[:, None] - cumulative), 0.0)
        * step_rows
    )
    weighted = (trailing.T[:, :, None] * x_heads.astype(F32)).astype(BF16)
    local_state = jnp.dot(
        b_rows.T, weighted.reshape(block_len, -1), preferred_element_type=F32
    )
    factor = jnp.where(segments[-1] == seg_before, jnp.exp(ending), 0.0)
    entry_gain = jnp.where((segments == seg_before)[None, :], jnp.exp(cumulative), 0.0)
    return (y_inner.reshape(block_len, -1), local_state, factor, entry_gain)


def spread_heads(values, width):
    return jnp.repeat(values, width, axis=-1)


def scan_shards(state, gain):
    rows = jnp.broadcast_to(gain[None, :], (8, gain.shape[0]))
    packed = jnp.concatenate([state, rows], axis=0)
    near = [along_seq(packed, step) for step in (1, 2, 3)]
    total, gains = packed[:STATE], packed[STATE : STATE + 1]
    for piece in near:
        total = total + gains * piece[:STATE]
        gains = gains * piece[STATE : STATE + 1]
    packed = jnp.concatenate([total, jnp.broadcast_to(gains, (8, gains.shape[1]))], axis=0)
    first, second = along_seq(packed, 1), along_seq(packed, 5)
    return first[:STATE] + first[STATE : STATE + 1] * second[:STATE]


def local(
    tokens,
    doc_lengths,
    value_weight,
    gate_weight,
    state_weight,
    step_weight,
    value_conv,
    state_conv,
    step_bias,
    log_rate,
):
    tok_dev = tokens.shape[0] * X * Y * C
    heads_here = step_weight.shape[1]
    tap_count = value_conv.shape[0]
    blocks = tok_dev // BLOCK
    cols = value_weight.shape[1]
    core = lax.axis_index("c")
    group = lax.axis_index("x") * 2 + lax.axis_index("y") // 2
    gathered = lax.all_gather(tokens, HEAD, axis=0, tiled=True)

    state_own = lax.dynamic_index_in_dim(state_weight, group, 0, keepdims=False)
    conv_own = lax.dynamic_index_in_dim(state_conv, group, 0, keepdims=False)
    state_half = jnp.where(core == 0, state_own[:, :STATE], state_own[:, STATE:])
    state_half = jnp.concatenate([state_half[:STATE], state_half[STATE:]], axis=1)
    step_rows = jnp.pad(step_weight.T, ((0, 8 - heads_here), (0, 0)))
    pack = jnp.concatenate([value_weight, state_half, step_rows, gate_weight], axis=0)
    both = lax.all_gather(pack, "yh", axis=0, tiled=False)
    first_rows = 256 + STATE + 8
    gate_all = lax.all_gather(both[:, first_rows:], "z", axis=0, tiled=False)
    held = ring_gather(both[:, :first_rows]).transpose(1, 0, 2, 3)

    depth = tokens.shape[1]
    value_all = held[:, :, :256].reshape(depth, cols)
    state_all = held[:, :, 256 : 256 + STATE]
    state_all = jnp.stack([state_all[..., :STATE], state_all[..., STATE:]], axis=2)
    state_all = state_all.reshape(depth, STATE)
    step_all = held[:, :, 256 + STATE :].transpose(0, 1, 3, 2).reshape(depth, 8)[:, :heads_here]

    half_proj = jnp.dot(gathered, state_all, preferred_element_type=F32).astype(BF16)
    other_proj = lax.ppermute(half_proj, "c", [(0, 1), (1, 0)])
    value_proj = jnp.dot(gathered, value_all, preferred_element_type=F32).astype(BF16)
    step_proj = jnp.dot(gathered, step_all, preferred_element_type=F32).astype(BF16)
    b_proj = jnp.where(core == 0, half_proj, other_proj)
    c_proj = jnp.where(core == 0, other_proj, half_proj)
    state_proj = jnp.concatenate([b_proj, c_proj], axis=1)

    rim_source = jnp.concatenate(
        [value_proj[-(tap_count - 1) :], state_proj[-(tap_count - 1) :]], axis=1
    )
    rim_rows = along_seq(rim_source, 1)
    value_ext = jnp.concatenate([rim_rows[:, :cols], value_proj], axis=0)
    state_ext = jnp.concatenate([rim_rows[:, cols:], state_proj], axis=0)
    starts = jnp.cumsum(doc_lengths) - doc_lengths
    positions = lax.axis_index(SEQ) * tok_dev + jnp.arange(-(tap_count - 1), tok_dev)
    seg_ext = segment_of(positions, starts)
    value_act = causal_conv(value_ext, value_conv, seg_ext, tok_dev)
    state_act = causal_conv(state_ext, conv_own, seg_ext, tok_dev)
    step_size = jax.nn.softplus(step_proj.astype(F32) + step_bias[None, :])
    decay_rate = -jnp.exp(log_rate)[None, :] * step_size
    seg_rows = seg_ext[tap_count - 1 :].reshape(blocks, BLOCK)
    seg_before = seg_ext[tap_count - 2 : tap_count - 2 + tok_dev : BLOCK]

    b_all = state_act[:, :STATE].reshape(blocks, BLOCK, STATE)
    c_all = state_act[:, STATE:].reshape(blocks, BLOCK, STATE)
    x_all = value_act.reshape(blocks, BLOCK, cols)
    decay_all = decay_rate.reshape(blocks, BLOCK, heads_here).transpose(0, 2, 1)
    step_all = step_size.reshape(blocks, BLOCK, heads_here).transpose(0, 2, 1)
    y_inner, local_state, factor, entry_gain = lax.map(
        lambda item: block_terms(*item),
        (b_all, c_all, x_all, decay_all, step_all, seg_rows, seg_before),
    )
    width = cols // heads_here
    factor = spread_heads(factor, width)
    running = jnp.zeros((STATE, cols), F32)
    gain = jnp.ones((cols,), F32)
    inside, gains = [], []
    for index in range(blocks):
        inside.append(running)
        gains.append(gain)
        running = factor[index][None, :] * running + local_state[index]
        gain = gain * factor[index]
    entering = scan_shards(running, gain)
    gate_full = gate_all.transpose(1, 0, 2, 3).reshape(depth, cols)
    gate_proj = jnp.dot(gathered, gate_full, preferred_element_type=F32).astype(BF16)
    outs = []
    for index in range(blocks):
        incoming = inside[index] + gains[index][None, :] * entering
        carried = jnp.dot(c_all[index].astype(F32), incoming, precision=lax.Precision.HIGHEST)
        carried = carried * spread_heads(entry_gain[index].T, width)
        total = y_inner[index] + carried + x_all[index].astype(F32)
        gating = jax.nn.silu(gate_proj[index * BLOCK : (index + 1) * BLOCK].astype(F32))
        outs.append((total * gating).astype(BF16))
    return jnp.concatenate(outs, axis=0)


def solution(mesh):
    grid = Mesh(mesh.devices.reshape(YH, Z, X, Y, C), SEQ + HEAD)
    return jax.shard_map(
        local,
        mesh=grid,
        in_specs=(
            P(SEQ + HEAD, None),
            P(),
            P(SEQ, HEAD),
            P(SEQ, HEAD),
            P(None, SEQ, None),
            P(SEQ, HEAD),
            P(None, HEAD),
            P(),
            P(HEAD),
            P(HEAD),
        ),
        out_specs=P(SEQ, HEAD),
        check_vma=False,
    )
```

```python
import functools

import jax
import jax.numpy as jnp
from jax import lax
from jax.experimental import pallas as pl
from jax.experimental.pallas import tpu as pltpu
from jax.sharding import Mesh
from jax.sharding import PartitionSpec as P

HEADS = 128
GROUPS = 8
BLOCK = 256
STATE = 128
WIDTH = 64
YH, Z, X, Y, C = 2, 8, 4, 4, 2
SEQ = ("yh", "z")
HEAD = ("x", "y", "c")
F32 = jnp.float32
BF16 = jnp.bfloat16
MIB = 1024 * 1024
FAR = -1e30


def ring(count, step):
    return [(i, (i + step) % count) for i in range(count)]


def along_seq(value, step):
    return lax.ppermute(value, SEQ, [(i, i + step) for i in range(YH * Z - step)])


def ring_gather(block):
    pieces = [(0, 0, block)]
    right = left = block
    for step in range(1, 4):
        right = lax.ppermute(right, "z", ring(Z, 1))
        left = lax.ppermute(left, "z", ring(Z, -1))
        pieces += [(Z - step, 0, right), (step, 0, left)]
    right = lax.ppermute(right[:1], "z", ring(Z, 1))
    left = lax.ppermute(left[1:], "z", ring(Z, -1))
    return pieces + [(4, 0, right), (4, 1, left)]


def call(
    kernel, grid, in_specs, out_specs, out_shape, scratch=(), prefetch=0, cost=None, room=12
):
    return pl.pallas_call(
        kernel,
        grid_spec=pltpu.PrefetchScalarGridSpec(
            num_scalar_prefetch=prefetch,
            grid=grid,
            in_specs=in_specs,
            out_specs=out_specs,
            scratch_shapes=scratch,
        ),
        out_shape=out_shape,
        compiler_params=pltpu.CompilerParams(
            vmem_limit_bytes=room * MIB, dimension_semantics=("arbitrary",) * len(grid)
        ),
        cost_estimate=cost,
    )


def whole(shape):
    return pl.BlockSpec(shape, lambda *_: (0,) * len(shape))


def rows_of(shape):
    return pl.BlockSpec(shape, lambda i, *_: (i,) + (0,) * (len(shape) - 1))


def assemble_kernel(layout, scalars, *refs):
    count = len(layout)
    pieces, swapped, out = refs[:count], refs[count : 2 * count], refs[2 * count]
    z, core = scalars[0], scalars[1]
    for (offset, first, yh_count), piece, other in zip(layout, pieces, swapped):
        source = lax.rem(z + offset, Z)
        for local_yh in range(yh_count):
            start = pl.multiple_of(((first + local_yh) * Z + source) * 256, 256)
            out[pl.ds(start, 256), 0:256] = piece[local_yh, 0:256, :]
            own = pl.multiple_of(start + core * 128, 128)
            its = pl.multiple_of(start + (1 - core) * 128, 128)
            out[pl.ds(own, 128), 256:512] = piece[local_yh, 256:384, :]
            out[pl.ds(its, 128), 256:512] = other[local_yh, :, :]
            steps = piece[local_yh, 384:392, :].astype(F32).T
            steps = jnp.concatenate([steps, jnp.zeros((256, 120), F32)], axis=1)
            out[pl.ds(start, 256), 512:640] = steps.astype(BF16)


def project_kernel(tok_ref, w_ref, out_ref):
    out_ref[...] = jnp.dot(
        tok_ref[...], w_ref[...], preferred_element_type=F32
    ).astype(BF16)


def gate_kernel(tok_ref, w_ref, out_ref):
    weights = jnp.concatenate([w_ref[z, yh] for yh in range(YH) for z in range(Z)], axis=0)
    proj = jnp.dot(tok_ref[...], weights, preferred_element_type=F32).astype(BF16)
    out_ref[...] = jax.nn.silu(proj.astype(F32))


def spread(columns):
    rows = columns.shape[0]
    lane = lax.broadcasted_iota(jnp.int32, (rows, 128), 1)
    wide = [jnp.broadcast_to(columns[:, h : h + 1], (rows, 128)) for h in range(4)]
    return jnp.concatenate(
        [jnp.where(lane < WIDTH, wide[0], wide[1]), jnp.where(lane < WIDTH, wide[2], wide[3])],
        axis=1,
    )


def doc_start(starts, positions):
    found = jnp.zeros(positions.shape, jnp.int32)
    for j in range(16):
        found = jnp.where(starts[j] <= positions, starts[j], found)
    return found


def state_kernel(
    starts, base, proj_ref, rim_ref, taps_ref, small_ref,
    act_ref, cum_ref, step_ref, inside_ref, gain_ref, packed_ref,
    ext, running, gains,
):
    block = pl.program_id(0)
    first = base[0] + block * BLOCK

    @pl.when(block == 0)
    def _():
        ext[0:8, :] = rim_ref[...].astype(F32)
        running[...] = jnp.zeros_like(running)
        gains[...] = jnp.ones_like(gains)

    proj = proj_ref[...]
    tile = proj[:, 0:512].astype(F32)
    ext[8 : 8 + BLOCK, :] = tile
    positions = first + lax.broadcasted_iota(jnp.int32, (BLOCK, 128), 0)
    start = doc_start(starts, positions)
    depth = (positions - start)[:, 0:1]
    summed = taps_ref[3:4, :] * tile
    for lag in (1, 2, 3):
        window = ext[8 - lag : 8 - lag + BLOCK, :]
        summed = summed + jnp.where(depth >= lag, taps_ref[3 - lag : 4 - lag, :] * window, 0.0)
    act = jax.nn.silu(summed).astype(BF16)
    act_ref[...] = act
    ext[0:8, :] = tile[BLOCK - 8 :, :]

    step = jax.nn.softplus(proj[:, 512:640].astype(F32) + small_ref[0:1, :])
    decay = -jnp.exp(small_ref[1:2, :]) * step
    tri = (
        lax.broadcasted_iota(jnp.int32, (BLOCK, BLOCK), 1)
        <= lax.broadcasted_iota(jnp.int32, (BLOCK, BLOCK), 0)
    ).astype(F32)
    cumulative = jnp.dot(
        tri, decay, preferred_element_type=F32, precision=lax.Precision.HIGHEST
    )
    cum_ref[...] = cumulative
    step_ref[...] = step
    ending = cumulative[BLOCK - 1 : BLOCK, :]
    last_start = start[BLOCK - 1 : BLOCK, :]
    trailing = jnp.where(positions >= last_start, jnp.exp(ending - cumulative) * step, 0.0)
    weighted = (spread(trailing) * act[:, 0:256].astype(F32)).astype(BF16)
    local_state = lax.dot_general(
        act[:, 256:384], weighted, (((0,), (0,)), ((), ())), preferred_element_type=F32
    )
    factor = jnp.where(last_start < first, jnp.exp(ending), 0.0)
    factor = spread(jnp.broadcast_to(factor, (8, 128)))
    inside_ref[0] = running[...]
    gain_ref[0] = gains[...]
    running[...] = factor[0:1, :] * running[...] + local_state
    gains[...] = gains[...] * factor

    @pl.when(block == pl.num_programs(0) - 1)
    def _():
        packed_ref[0:STATE, :] = running[...].astype(BF16)
        high = gains[...].astype(BF16)
        low = (gains[...] - high.astype(F32)).astype(BF16)
        packed_ref[STATE : STATE + 16, :] = jnp.concatenate([high, low], axis=0)


def block_kernel(
    starts, base, act_ref, cum_ref, step_ref, inside_ref, gain_ref, y_ref, reach_ref
):
    first = base[0] + pl.program_id(0) * BLOCK
    act = act_ref[...]
    x_act, b_act, c_act = act[:, 0:256], act[:, 256:384], act[:, 384:512]
    cumulative = cum_ref[...]
    cum_rows, step_rows = cumulative.T, step_ref[...].T
    products = lax.dot_general(
        c_act, b_act, (((1,), (1,)), ((), ())), preferred_element_type=F32
    )
    start = doc_start(starts, first + lax.broadcasted_iota(jnp.int32, (BLOCK, 128), 0))
    row = lax.broadcasted_iota(jnp.int32, (BLOCK, BLOCK), 0)
    column = lax.broadcasted_iota(jnp.int32, (BLOCK, BLOCK), 1)
    allowed = (column <= row) & (first + column >= start[:, 0:1])
    parts = []
    for h in range(4):
        gap = cumulative[:, h : h + 1] - cum_rows[h : h + 1, :]
        decay = jnp.exp(jnp.where(allowed, gap, FAR))
        scores = (products * decay * step_rows[h : h + 1, :]).astype(BF16)
        parts.append(
            jnp.dot(scores, x_act[:, h * WIDTH : (h + 1) * WIDTH], preferred_element_type=F32)
        )
    y_inner = jnp.concatenate(parts, axis=1)
    reach = spread(jnp.where(start < first, jnp.exp(cumulative), 0.0))
    inside = inside_ref[0]
    high = inside.astype(BF16)
    low = (inside - high.astype(F32)).astype(BF16)
    carried = jnp.dot(c_act, high, preferred_element_type=F32) + jnp.dot(
        c_act, low, preferred_element_type=F32
    )
    y_ref[...] = y_inner + reach * carried + x_act.astype(F32)
    reach_ref[...] = reach * gain_ref[0, 0:1, :]


def gain_of(packed):
    return packed[STATE : STATE + 8].astype(F32) + packed[STATE + 8 : STATE + 16].astype(F32)


def near_kernel(own_ref, one_ref, two_ref, three_ref, out_ref):
    own = own_ref[...]
    total, gain = own[0:STATE].astype(F32), gain_of(own)
    for ref in (one_ref, two_ref, three_ref):
        piece = ref[...]
        total = total + gain[0:1] * piece[0:STATE].astype(F32)
        gain = gain * gain_of(piece)
    high = gain.astype(BF16)
    low = (gain - high.astype(F32)).astype(BF16)
    out_ref[0:STATE, :] = total.astype(BF16)
    out_ref[STATE : STATE + 16, :] = jnp.concatenate([high, low], axis=0)


def finish_kernel(first_ref, second_ref, act_ref, y_ref, reach_ref, gate_ref, out_ref):
    first, second = first_ref[...], second_ref[...]
    gain = gain_of(first)[0:1]
    entering = first[0:STATE].astype(F32) + gain * second[0:STATE].astype(F32)
    carried = jnp.dot(act_ref[...], entering.astype(BF16), preferred_element_type=F32)
    out_ref[...] = ((y_ref[...] + reach_ref[...] * carried) * gate_ref[...]).astype(BF16)


def shape(dims, dtype):
    return jax.ShapeDtypeStruct(dims, dtype)


def work(flops, moved, exps=0):
    return pl.CostEstimate(flops=flops, bytes_accessed=moved, transcendentals=exps)


def run_assemble(pieces, swapped, scalars):
    layout = tuple((offset, first, piece.shape[0]) for offset, first, piece in pieces)
    arrays = [piece for _, _, piece in pieces]
    return call(
        functools.partial(assemble_kernel, layout),
        (1,),
        [whole(a.shape) for a in arrays] + [whole(a.shape) for a in swapped],
        whole((4096, 640)),
        shape((4096, 640), BF16),
        prefetch=1,
        cost=work(0, 12 << 20),
        room=24,
    )(scalars, *arrays, *swapped)


def run_project(gathered, weights):
    rows, depth = gathered.shape
    cols = weights.shape[1]
    return call(
        project_kernel,
        (rows // 256,),
        [rows_of((256, depth)), whole((depth, cols))],
        rows_of((256, cols)),
        shape((rows, cols), BF16),
        cost=work(2 * rows * depth * cols, 14 << 20),
        room=48,
    )(gathered, weights)


def run_gate(gathered, gate_all):
    rows, depth = gathered.shape
    return call(
        gate_kernel,
        (rows // 256,),
        [rows_of((256, depth)), whole(gate_all.shape)],
        rows_of((256, 256)),
        shape((rows, 256), F32),
        cost=work(2 * rows * depth * 256, 11 << 20),
        room=48,
    )(gathered, gate_all)


def run_state(starts, base, proj, rim, taps, small):
    rows = proj.shape[0]
    blocks = rows // BLOCK
    return call(
        state_kernel,
        (blocks,),
        [rows_of((BLOCK, 640)), whole((8, 512)), whole((4, 512)), whole((8, 128))],
        [
            rows_of((BLOCK, 512)),
            rows_of((BLOCK, 128)),
            rows_of((BLOCK, 128)),
            rows_of((1, STATE, 256)),
            rows_of((1, 8, 256)),
            whole((STATE + 16, 256)),
        ],
        [
            shape((rows, 512), BF16),
            shape((rows, 128), F32),
            shape((rows, 128), F32),
            shape((blocks, STATE, 256), F32),
            shape((blocks, 8, 256), F32),
            shape((STATE + 16, 256), BF16),
        ],
        scratch=[
            pltpu.VMEM((8 + BLOCK, 512), F32),
            pltpu.VMEM((STATE, 256), F32),
            pltpu.VMEM((8, 256), F32),
        ],
        prefetch=2,
        cost=work(2 * rows * 128 * 256, 4 << 20, rows * 1024),
    )(starts, base, proj, rim, taps, small)


def run_blocks(starts, base, act, cum, step, inside, gains):
    rows = act.shape[0]
    blocks = rows // BLOCK
    return call(
        block_kernel,
        (blocks,),
        [
            rows_of((BLOCK, 512)),
            rows_of((BLOCK, 128)),
            rows_of((BLOCK, 128)),
            rows_of((1, STATE, 256)),
            rows_of((1, 8, 256)),
        ],
        [rows_of((BLOCK, 256)), rows_of((BLOCK, 256))],
        [shape((rows, 256), F32), shape((rows, 256), F32)],
        prefetch=2,
        cost=work(2 * rows * 256 * 1024, 5 << 20, rows * 1280),
    )(starts, base, act, cum, step, inside, gains)


def run_near(pieces):
    return call(
        near_kernel,
        (1,),
        [whole(p.shape) for p in pieces],
        whole(pieces[0].shape),
        shape(pieces[0].shape, BF16),
        cost=work(1 << 18, 1 << 19),
    )(*pieces)


def run_finish(first, second, act, y, reach, gate):
    rows = y.shape[0]
    return call(
        finish_kernel,
        (rows // BLOCK,),
        [
            whole(first.shape),
            whole(second.shape),
            pl.BlockSpec((BLOCK, 128), lambda i: (i, 3)),
            rows_of((BLOCK, 256)),
            rows_of((BLOCK, 256)),
            rows_of((BLOCK, 256)),
        ],
        rows_of((BLOCK, 256)),
        shape((rows, 256), BF16),
        cost=work(2 * rows * 128 * 256, 4 << 20),
    )(first, second, act, y, reach, gate)


def local(
    tokens,
    doc_lengths,
    value_weight,
    gate_weight,
    state_weight,
    step_weight,
    value_conv,
    state_conv,
    step_bias,
    log_rate,
):
    tok_dev = tokens.shape[0] * X * Y * C
    heads_here = step_weight.shape[1]
    core = lax.axis_index("c")
    z = lax.axis_index("z")
    group = lax.axis_index("x") * 2 + lax.axis_index("y") // 2
    gathered = lax.all_gather(tokens, HEAD, axis=0, tiled=True)

    state_half = lax.dynamic_slice(state_weight, (group, core * 128, 0), (1, 128, 256))[0]
    conv_own = lax.dynamic_index_in_dim(state_conv, group, 0, keepdims=False)
    step_rows = jnp.pad(step_weight.T, ((0, 8 - heads_here), (0, 0)))
    pack = jnp.concatenate([value_weight, state_half, step_rows, gate_weight], axis=0)
    both = lax.all_gather(pack, "yh", axis=0, tiled=False)
    pieces = ring_gather(both[:, :392])
    halves = jnp.concatenate([piece[:, 256:384] for _, _, piece in pieces], axis=0)
    halves = lax.ppermute(halves, "c", [(0, 1), (1, 0)])
    swapped, at = [], 0
    for _, _, piece in pieces:
        swapped.append(halves[at : at + piece.shape[0]])
        at += piece.shape[0]
    scalars = jnp.stack([z, core]).astype(jnp.int32)
    weights = run_assemble(pieces, swapped, scalars)
    gate_part, gathered, weights = lax.optimization_barrier((both[:, 392:], gathered, weights))
    gate_all = lax.all_gather(gate_part, "z", axis=0, tiled=False)
    proj = run_project(gathered, weights)
    rim = along_seq(proj[-8:, :512], 1)

    starts = (jnp.cumsum(doc_lengths) - doc_lengths).astype(jnp.int32)
    base = (lax.axis_index(SEQ) * tok_dev).astype(jnp.int32).reshape(1)
    taps = jnp.concatenate([value_conv, conv_own], axis=1)
    small = jnp.pad(jnp.stack([step_bias, log_rate]), ((0, 6), (0, 128 - heads_here)))
    act, cum, step, inside, gains, packed = run_state(starts, base, proj, rim, taps, small)
    near = run_near([packed] + [along_seq(packed, hop) for hop in (1, 2, 3)])
    y, reach = run_blocks(starts, base, act, cum, step, inside, gains)
    first, second = along_seq(near, 1), along_seq(near, 5)
    gate = run_gate(gathered, gate_all)
    return run_finish(first, second, act, y, reach, gate)


def solution(mesh):
    grid = Mesh(mesh.devices.reshape(YH, Z, X, Y, C), SEQ + HEAD)
    return jax.shard_map(
        local,
        mesh=grid,
        in_specs=(
            P(SEQ + HEAD, None),
            P(),
            P(SEQ, HEAD),
            P(SEQ, HEAD),
            P(None, SEQ, None),
            P(SEQ, HEAD),
            P(None, HEAD),
            P(),
            P(HEAD),
            P(HEAD),
        ),
        out_specs=P(SEQ, HEAD),
        check_vma=False,
    )
```

```python
import functools

import jax
import jax.numpy as jnp
from jax import lax
from jax.experimental import pallas as pl
from jax.experimental.pallas import tpu as pltpu
from jax.sharding import Mesh
from jax.sharding import PartitionSpec as P

HEADS = 128
GROUPS = 8
BLOCK = 256
STATE = 128
WIDTH = 64
YH, Z, X, Y, C = 2, 8, 4, 4, 2
SEQ = ("yh", "z")
HEAD = ("x", "y", "c")
F32 = jnp.float32
BF16 = jnp.bfloat16
MIB = 1024 * 1024
FAR = -1e30


def ring(count, step):
    return [(i, (i + step) % count) for i in range(count)]


def along_seq(value, step):
    return lax.ppermute(value, SEQ, [(i, i + step) for i in range(YH * Z - step)])


def ring_gather(block):
    pieces = [(0, 0, block)]
    right = left = block
    for step in range(1, 4):
        right = lax.ppermute(right, "z", ring(Z, 1))
        left = lax.ppermute(left, "z", ring(Z, -1))
        pieces += [(Z - step, 0, right), (step, 0, left)]
    right = lax.ppermute(right[:1], "z", ring(Z, 1))
    left = lax.ppermute(left[1:], "z", ring(Z, -1))
    return pieces + [(4, 0, right), (4, 1, left)]


def call(
    kernel, grid, in_specs, out_specs, out_shape, scratch=(), prefetch=0, cost=None, room=12,
    aliases=None,
):
    return pl.pallas_call(
        kernel,
        grid_spec=pltpu.PrefetchScalarGridSpec(
            num_scalar_prefetch=prefetch,
            grid=grid,
            in_specs=in_specs,
            out_specs=out_specs,
            scratch_shapes=scratch,
        ),
        out_shape=out_shape,
        input_output_aliases=aliases or {},
        compiler_params=pltpu.CompilerParams(
            vmem_limit_bytes=room * MIB, dimension_semantics=("arbitrary",) * len(grid)
        ),
        cost_estimate=cost,
    )


def whole(shape):
    return pl.BlockSpec(shape, lambda *_: (0,) * len(shape))


def in_hbm(value):
    return pltpu.with_memory_space_constraint(value, pltpu.HBM)


def held(_):
    return pl.BlockSpec(memory_space=pltpu.VMEM)


def rows_of(shape):
    return pl.BlockSpec(shape, lambda i, *_: (i,) + (0,) * (len(shape) - 1))


def first_kernel(layout, scalars, tok_ref, *refs):
    pieces, other, proj_ref, out = refs[:-3], refs[-3], refs[-2], refs[-1]
    z, core = scalars[0], scalars[1]
    count = 0
    for (offset, first, yh_count), piece in zip(layout, pieces):
        source = lax.rem(z + offset, Z)
        for local_yh in range(yh_count):
            start = pl.multiple_of(((first + local_yh) * Z + source) * 256, 256)
            out[pl.ds(start, 256), 0:256] = piece[local_yh, 0:256, :]
            own = pl.multiple_of(start + core * 128, 128)
            its = pl.multiple_of(start + (1 - core) * 128, 128)
            out[pl.ds(own, 128), 256:512] = piece[local_yh, 256:384, :]
            out[pl.ds(its, 128), 256:512] = other[count, :, :]
            count += 1
            steps = piece[local_yh, 384:392, :].astype(F32).T
            steps = jnp.concatenate([steps, jnp.zeros((256, 120), F32)], axis=1)
            out[pl.ds(start, 256), 512:640] = steps.astype(BF16)
    project(tok_ref, out, proj_ref)


def project(tok_ref, w_ref, out_ref):
    out_ref[...] = jnp.dot(
        tok_ref[...], w_ref[...], preferred_element_type=F32
    ).astype(BF16)


def rest_kernel(tok_ref, w_ref, _, out_ref):
    project(tok_ref, w_ref, out_ref)


def spread(columns):
    rows = columns.shape[0]
    lane = lax.broadcasted_iota(jnp.int32, (rows, 128), 1)
    wide = [jnp.broadcast_to(columns[:, h : h + 1], (rows, 128)) for h in range(4)]
    return jnp.concatenate(
        [jnp.where(lane < WIDTH, wide[0], wide[1]), jnp.where(lane < WIDTH, wide[2], wide[3])],
        axis=1,
    )


def doc_start(starts, positions):
    found = jnp.zeros(positions.shape, jnp.int32)
    for j in range(16):
        found = jnp.where(starts[j] <= positions, starts[j], found)
    return found


def state_kernel(
    starts, base, proj_ref, rim_ref, taps_ref, small_ref,
    act_ref, cum_ref, step_ref, inside_ref, gain_ref, packed_ref,
    ext, running, gains,
):
    block = pl.program_id(0)
    first = base[0] + block * BLOCK

    @pl.when(block == 0)
    def _():
        ext[0:8, :] = rim_ref[...].astype(F32)
        running[...] = jnp.zeros_like(running)
        gains[...] = jnp.ones_like(gains)

    proj = proj_ref[...]
    tile = proj[:, 0:512].astype(F32)
    ext[8 : 8 + BLOCK, :] = tile
    positions = first + lax.broadcasted_iota(jnp.int32, (BLOCK, 128), 0)
    start = doc_start(starts, positions)
    depth = (positions - start)[:, 0:1]
    summed = taps_ref[3:4, :] * tile
    for lag in (1, 2, 3):
        window = ext[8 - lag : 8 - lag + BLOCK, :]
        summed = summed + jnp.where(depth >= lag, taps_ref[3 - lag : 4 - lag, :] * window, 0.0)
    act = jax.nn.silu(summed).astype(BF16)
    act_ref[...] = act
    ext[0:8, :] = tile[BLOCK - 8 :, :]

    step = jax.nn.softplus(proj[:, 512:640].astype(F32) + small_ref[0:1, :])
    decay = -jnp.exp(small_ref[1:2, :]) * step
    tri = (
        lax.broadcasted_iota(jnp.int32, (BLOCK, BLOCK), 1)
        <= lax.broadcasted_iota(jnp.int32, (BLOCK, BLOCK), 0)
    ).astype(F32)
    cumulative = jnp.dot(
        tri, decay, preferred_element_type=F32, precision=lax.Precision.HIGHEST
    )
    cum_ref[...] = cumulative
    step_ref[...] = step
    ending = cumulative[BLOCK - 1 : BLOCK, :]
    last_start = start[BLOCK - 1 : BLOCK, :]
    trailing = jnp.where(positions >= last_start, jnp.exp(ending - cumulative) * step, 0.0)
    weighted = (spread(trailing) * act[:, 0:256].astype(F32)).astype(BF16)
    local_state = lax.dot_general(
        act[:, 256:384], weighted, (((0,), (0,)), ((), ())), preferred_element_type=F32
    )
    factor = jnp.where(last_start < first, jnp.exp(ending), 0.0)
    factor = spread(jnp.broadcast_to(factor, (8, 128)))
    inside_ref[0] = running[...]
    gain_ref[0] = gains[...]
    running[...] = factor[0:1, :] * running[...] + local_state
    gains[...] = gains[...] * factor

    @pl.when(block == pl.num_programs(0) - 1)
    def _():
        packed_ref[0:STATE, :] = running[...].astype(BF16)
        high = gains[...].astype(BF16)
        low = (gains[...] - high.astype(F32)).astype(BF16)
        packed_ref[STATE : STATE + 16, :] = jnp.concatenate([high, low], axis=0)


def block_kernel(
    starts, base, act_ref, cum_ref, step_ref, inside_ref, gain_ref, y_ref, reach_ref
):
    first = base[0] + pl.program_id(0) * BLOCK
    act = act_ref[...]
    x_act, b_act, c_act = act[:, 0:256], act[:, 256:384], act[:, 384:512]
    cumulative = cum_ref[...]
    cum_rows, step_rows = cumulative.T, step_ref[...].T
    products = lax.dot_general(
        c_act, b_act, (((1,), (1,)), ((), ())), preferred_element_type=F32
    )
    start = doc_start(starts, first + lax.broadcasted_iota(jnp.int32, (BLOCK, 128), 0))
    row = lax.broadcasted_iota(jnp.int32, (BLOCK, BLOCK), 0)
    column = lax.broadcasted_iota(jnp.int32, (BLOCK, BLOCK), 1)
    allowed = (column <= row) & (first + column >= start[:, 0:1])
    parts = []
    for h in range(4):
        gap = cumulative[:, h : h + 1] - cum_rows[h : h + 1, :]
        decay = jnp.exp(jnp.where(allowed, gap, FAR))
        scores = (products * decay * step_rows[h : h + 1, :]).astype(BF16)
        parts.append(
            jnp.dot(scores, x_act[:, h * WIDTH : (h + 1) * WIDTH], preferred_element_type=F32)
        )
    y_inner = jnp.concatenate(parts, axis=1)
    reach = spread(jnp.where(start < first, jnp.exp(cumulative), 0.0))
    inside = inside_ref[0]
    high = inside.astype(BF16)
    low = (inside - high.astype(F32)).astype(BF16)
    carried = jnp.dot(c_act, high, preferred_element_type=F32) + jnp.dot(
        c_act, low, preferred_element_type=F32
    )
    y_ref[...] = y_inner + reach * carried + x_act.astype(F32)
    reach_ref[...] = reach * gain_ref[0, 0:1, :]


def gain_of(packed):
    return packed[STATE : STATE + 8].astype(F32) + packed[STATE + 8 : STATE + 16].astype(F32)


def carry_kernel(own_ref, before_ref, out_ref):
    own, before = own_ref[...], before_ref[...]
    total = own[0:STATE].astype(F32) + gain_of(own)[0:1] * before[0:STATE].astype(F32)
    out_ref[0:STATE, :] = total.astype(BF16)
    out_ref[STATE : STATE + 16, :] = own[STATE : STATE + 16]


def finish_kernel(
    scalars, before_ref, shards_ref, act_ref, y_ref, reach_ref, tok_ref, w_ref, out_ref,
    entering, weights,
):
    @pl.when(pl.program_id(0) == 0)
    def _():
        z = scalars[0]
        state = jnp.zeros((STATE, 256), F32)
        for k in range(Z - 1):
            piece = shards_ref[k]
            later = gain_of(piece)[0:1] * state + piece[0:STATE].astype(F32)
            state = jnp.where(k < z, later, state)
        entering[...] = (state + before_ref[0:STATE, :].astype(F32)).astype(BF16)
        for k in range(Z):
            for yh in range(YH):
                weights[pl.ds((yh * Z + k) * 256, 256), :] = w_ref[k, yh]

    gate = jnp.dot(tok_ref[...], weights[...], preferred_element_type=F32).astype(BF16)
    carried = jnp.dot(act_ref[...], entering[...], preferred_element_type=F32)
    total = y_ref[...] + reach_ref[...] * carried
    out_ref[...] = (total * jax.nn.silu(gate.astype(F32))).astype(BF16)


def shape(dims, dtype):
    return jax.ShapeDtypeStruct(dims, dtype)


def work(flops, moved, exps=0):
    return pl.CostEstimate(flops=flops, bytes_accessed=moved, transcendentals=exps)


def run_first(gathered, pieces, swapped, scalars):
    rows, depth = gathered.shape
    layout = tuple((offset, first, piece.shape[0]) for offset, first, piece in pieces)
    arrays = [in_hbm(piece) for _, _, piece in pieces] + [in_hbm(swapped)]
    last = rows // BLOCK - 1
    return call(
        functools.partial(first_kernel, layout),
        (1,),
        [pl.BlockSpec((BLOCK, depth), lambda *_: (last, 0))] + [whole(a.shape) for a in arrays],
        [pl.BlockSpec((BLOCK, 640), lambda *_: (last, 0)), held(None)],
        [shape((rows, 640), BF16), shape((depth, 640), BF16)],
        prefetch=1,
        cost=work(2 * BLOCK * depth * 640, 12 << 20),
        room=24,
    )(scalars, gathered, *arrays)


def run_rest(gathered, weights, proj):
    rows, depth = gathered.shape
    count = rows // BLOCK - 1
    return call(
        rest_kernel,
        (count,),
        [rows_of((BLOCK, depth)), held(weights), pl.BlockSpec(memory_space=pl.ANY)],
        rows_of((BLOCK, 640)),
        shape((rows, 640), BF16),
        cost=work(2 * count * BLOCK * depth * 640, 8 << 20),
        room=16,
        aliases={2: 0},
    )(gathered, weights, proj)


def run_state(starts, base, proj, rim, taps, small):
    rows = proj.shape[0]
    blocks = rows // BLOCK
    return call(
        state_kernel,
        (blocks,),
        [rows_of((BLOCK, 640)), whole((8, 512)), whole((4, 512)), whole((8, 128))],
        [
            rows_of((BLOCK, 512)),
            rows_of((BLOCK, 128)),
            rows_of((BLOCK, 128)),
            rows_of((1, STATE, 256)),
            rows_of((1, 8, 256)),
            whole((STATE + 16, 256)),
        ],
        [
            shape((rows, 512), BF16),
            shape((rows, 128), F32),
            shape((rows, 128), F32),
            shape((blocks, STATE, 256), F32),
            shape((blocks, 8, 256), F32),
            shape((STATE + 16, 256), BF16),
        ],
        scratch=[
            pltpu.VMEM((8 + BLOCK, 512), F32),
            pltpu.VMEM((STATE, 256), F32),
            pltpu.VMEM((8, 256), F32),
        ],
        prefetch=2,
        cost=work(2 * rows * 128 * 256, 4 << 20, rows * 1024),
    )(starts, base, proj, rim, taps, small)


def run_blocks(starts, base, act, cum, step, inside, gains):
    rows = act.shape[0]
    blocks = rows // BLOCK
    return call(
        block_kernel,
        (blocks,),
        [
            rows_of((BLOCK, 512)),
            rows_of((BLOCK, 128)),
            rows_of((BLOCK, 128)),
            rows_of((1, STATE, 256)),
            rows_of((1, 8, 256)),
        ],
        [rows_of((BLOCK, 256)), rows_of((BLOCK, 256))],
        [pltpu.HBM((rows, 256), F32), pltpu.HBM((rows, 256), F32)],
        prefetch=2,
        cost=work(2 * rows * 256 * 1024, 5 << 20, rows * 1280),
    )(starts, base, act, cum, step, inside, gains)


def run_carry(own, before):
    return call(
        carry_kernel,
        (1,),
        [held(own), held(before)],
        held(own),
        shape(own.shape, BF16),
        cost=work(1 << 17, 1 << 18),
        room=4,
    )(own, before)


def run_finish(scalars, before, shards, act, y, reach, gathered, gate_all):
    rows, depth = gathered.shape
    return call(
        finish_kernel,
        (rows // BLOCK,),
        [
            held(before),
            held(shards),
            pl.BlockSpec((BLOCK, 128), lambda i, *_: (i, 3)),
            rows_of((BLOCK, 256)),
            rows_of((BLOCK, 256)),
            rows_of((BLOCK, depth)),
            whole(gate_all.shape),
        ],
        rows_of((BLOCK, 256)),
        shape((rows, 256), BF16),
        scratch=[pltpu.VMEM((STATE, 256), BF16), pltpu.VMEM((depth, 256), BF16)],
        prefetch=1,
        cost=work(2 * rows * (128 + depth) * 256, 13 << 20),
        room=20,
    )(scalars, before, shards, act, y, reach, gathered, gate_all)


def local(
    tokens,
    doc_lengths,
    value_weight,
    gate_weight,
    state_weight,
    step_weight,
    value_conv,
    state_conv,
    step_bias,
    log_rate,
):
    tok_dev = tokens.shape[0] * X * Y * C
    heads_here = step_weight.shape[1]
    core = lax.axis_index("c")
    z = lax.axis_index("z")
    group = lax.axis_index("x") * 2 + lax.axis_index("y") // 2
    gathered = lax.all_gather(tokens, HEAD, axis=0, tiled=True)

    state_half = lax.dynamic_slice(state_weight, (group, core * 128, 0), (1, 128, 256))[0]
    conv_own = lax.dynamic_index_in_dim(state_conv, group, 0, keepdims=False)
    step_rows = jnp.pad(step_weight.T, ((0, 8 - heads_here), (0, 0)))
    pack = jnp.concatenate([value_weight, state_half, step_rows, gate_weight], axis=0)
    both = lax.all_gather(pack, "yh", axis=0, tiled=False)
    pieces = ring_gather(both[:, :392])
    halves = jnp.concatenate([piece[:, 256:384] for _, _, piece in pieces], axis=0)
    halves = lax.ppermute(halves, "c", [(0, 1), (1, 0)])
    scalars = jnp.stack([z, core]).astype(jnp.int32)
    gate_part, gathered, halves = lax.optimization_barrier((both[:, 392:], gathered, halves))
    gate_all = lax.all_gather(gate_part, "z", axis=0, tiled=False)
    gathered = in_hbm(gathered)
    proj, weights = run_first(gathered, pieces, halves, scalars)
    rim = along_seq(proj[-8:, :512], 1)
    proj = run_rest(gathered, weights, proj)

    starts = (jnp.cumsum(doc_lengths) - doc_lengths).astype(jnp.int32)
    base = (lax.axis_index(SEQ) * tok_dev).astype(jnp.int32).reshape(1)
    taps = jnp.concatenate([value_conv, conv_own], axis=1)
    small = jnp.pad(jnp.stack([step_bias, log_rate]), ((0, 6), (0, 128 - heads_here)))
    act, cum, step, inside, gains, packed = run_state(starts, base, proj, rim, taps, small)
    before = lax.ppermute(packed, SEQ, [(Z - 1, Z)])
    y, reach = run_blocks(starts, base, act, cum, step, inside, gains)
    carried = run_carry(packed, before)
    shards = lax.all_gather(carried, "z", axis=0, tiled=False)
    return run_finish(
        scalars, before, shards, act, in_hbm(y), in_hbm(reach), gathered, in_hbm(gate_all)
    )


def solution(mesh):
    grid = Mesh(mesh.devices.reshape(YH, Z, X, Y, C), SEQ + HEAD)
    return jax.shard_map(
        local,
        mesh=grid,
        in_specs=(
            P(SEQ + HEAD, None),
            P(),
            P(SEQ, HEAD),
            P(SEQ, HEAD),
            P(None, SEQ, None),
            P(SEQ, HEAD),
            P(None, HEAD),
            P(),
            P(HEAD),
            P(HEAD),
        ),
        out_specs=P(SEQ, HEAD),
        check_vma=False,
    )
```

```python
import functools

import jax
import jax.numpy as jnp
from jax import lax
from jax.experimental import pallas as pl
from jax.experimental.pallas import tpu as pltpu
from jax.sharding import Mesh
from jax.sharding import PartitionSpec as P

HEADS = 128
GROUPS = 8
BLOCK = 256
STATE = 128
WIDTH = 64
YH, Z, X, Y, C = 2, 8, 4, 4, 2
SEQ = ("yh", "z")
HEAD = ("x", "y", "c")
F32 = jnp.float32
BF16 = jnp.bfloat16
MIB = 1024 * 1024
FAR = -1e30
CHUNK = 1024


def ring(count, step):
    return [(i, (i + step) % count) for i in range(count)]


def along_seq(value, step):
    return lax.ppermute(value, SEQ, [(i, i + step) for i in range(YH * Z - step)])


def ring_gather(block):
    pieces = [(0, 0, block)]
    right = left = block
    for step in range(1, 4):
        right = lax.ppermute(right, "z", ring(Z, 1))
        left = lax.ppermute(left, "z", ring(Z, -1))
        pieces += [(Z - step, 0, right), (step, 0, left)]
    right = lax.ppermute(right[:1], "z", ring(Z, 1))
    left = lax.ppermute(left[1:], "z", ring(Z, -1))
    return pieces + [(4, 0, right), (4, 1, left)]


def call(
    kernel, grid, in_specs, out_specs, out_shape, scratch=(), prefetch=0, cost=None, room=12,
    aliases=None,
):
    return pl.pallas_call(
        kernel,
        grid_spec=pltpu.PrefetchScalarGridSpec(
            num_scalar_prefetch=prefetch,
            grid=grid,
            in_specs=in_specs,
            out_specs=out_specs,
            scratch_shapes=scratch,
        ),
        out_shape=out_shape,
        input_output_aliases=aliases or {},
        compiler_params=pltpu.CompilerParams(
            vmem_limit_bytes=room * MIB, dimension_semantics=("arbitrary",) * len(grid)
        ),
        cost_estimate=cost,
    )


def whole(shape):
    return pl.BlockSpec(shape, lambda *_: (0,) * len(shape))


def in_hbm(value):
    return pltpu.with_memory_space_constraint(value, pltpu.HBM)


def held(_):
    return pl.BlockSpec(memory_space=pltpu.VMEM)


def rows_of(shape):
    return pl.BlockSpec(shape, lambda i, *_: (i,) + (0,) * (len(shape) - 1))


def first_kernel(layout, scalars, tok_ref, *refs):
    pieces, other, proj_ref, out = refs[:-3], refs[-3], refs[-2], refs[-1]
    z, core = scalars[0], scalars[1]
    count = 0
    for (offset, first, yh_count), piece in zip(layout, pieces):
        source = lax.rem(z + offset, Z)
        for local_yh in range(yh_count):
            start = pl.multiple_of(((first + local_yh) * Z + source) * 256, 256)
            out[pl.ds(start, 256), 0:256] = piece[local_yh, 0:256, :]
            own = pl.multiple_of(start + core * 128, 128)
            its = pl.multiple_of(start + (1 - core) * 128, 128)
            out[pl.ds(own, 128), 256:512] = piece[local_yh, 256:384, :]
            out[pl.ds(its, 128), 256:512] = other[count, :, :]
            count += 1
            steps = piece[local_yh, 384:392, :].astype(F32).T
            steps = jnp.concatenate([steps, jnp.zeros((256, 120), F32)], axis=1)
            out[pl.ds(start, 256), 512:640] = steps.astype(BF16)
    project(tok_ref, out, proj_ref)


def project(tok_ref, w_ref, out_ref):
    out_ref[...] = jnp.dot(
        tok_ref[...], w_ref[...], preferred_element_type=F32
    ).astype(BF16)


def rest_kernel(tok_ref, w_ref, _, out_ref, total):
    step = pl.program_id(0)
    part = jnp.dot(
        tok_ref[...], w_ref[pl.ds(step * CHUNK, CHUNK), :], preferred_element_type=F32
    )

    @pl.when(step == 0)
    def _():
        total[...] = part

    @pl.when(step > 0)
    def _():
        total[...] += part

    @pl.when(step == pl.num_programs(0) - 1)
    def _():
        out_ref[...] = total[...].astype(BF16)


def spread(columns):
    rows = columns.shape[0]
    lane = lax.broadcasted_iota(jnp.int32, (rows, 128), 1)
    wide = [jnp.broadcast_to(columns[:, h : h + 1], (rows, 128)) for h in range(4)]
    return jnp.concatenate(
        [jnp.where(lane < WIDTH, wide[0], wide[1]), jnp.where(lane < WIDTH, wide[2], wide[3])],
        axis=1,
    )


def doc_start(starts, positions):
    found = jnp.zeros(positions.shape, jnp.int32)
    for j in range(16):
        found = jnp.where(starts[j] <= positions, starts[j], found)
    return found


def state_kernel(
    starts, base, proj_ref, rim_ref, taps_ref, small_ref,
    act_ref, cum_ref, step_ref, inside_ref, gain_ref, packed_ref,
    ext, running, gains,
):
    block = pl.program_id(0)
    first = base[0] + block * BLOCK

    @pl.when(block == 0)
    def _():
        ext[0:8, :] = rim_ref[...].astype(F32)
        running[...] = jnp.zeros_like(running)
        gains[...] = jnp.ones_like(gains)

    proj = proj_ref[...]
    tile = proj[:, 0:512].astype(F32)
    ext[8 : 8 + BLOCK, :] = tile
    positions = first + lax.broadcasted_iota(jnp.int32, (BLOCK, 128), 0)
    start = doc_start(starts, positions)
    depth = (positions - start)[:, 0:1]
    summed = taps_ref[3:4, :] * tile
    for lag in (1, 2, 3):
        window = ext[8 - lag : 8 - lag + BLOCK, :]
        summed = summed + jnp.where(depth >= lag, taps_ref[3 - lag : 4 - lag, :] * window, 0.0)
    act = jax.nn.silu(summed).astype(BF16)
    act_ref[...] = act
    ext[0:8, :] = tile[BLOCK - 8 :, :]

    step = jax.nn.softplus(proj[:, 512:640].astype(F32) + small_ref[0:1, :])
    decay = -jnp.exp(small_ref[1:2, :]) * step
    tri = (
        lax.broadcasted_iota(jnp.int32, (BLOCK, BLOCK), 1)
        <= lax.broadcasted_iota(jnp.int32, (BLOCK, BLOCK), 0)
    ).astype(F32)
    cumulative = jnp.dot(
        tri, decay, preferred_element_type=F32, precision=lax.Precision.HIGHEST
    )
    cum_ref[...] = cumulative
    step_ref[...] = step
    ending = cumulative[BLOCK - 1 : BLOCK, :]
    last_start = start[BLOCK - 1 : BLOCK, :]
    trailing = jnp.where(positions >= last_start, jnp.exp(ending - cumulative) * step, 0.0)
    weighted = (spread(trailing) * act[:, 0:256].astype(F32)).astype(BF16)
    local_state = lax.dot_general(
        act[:, 256:384], weighted, (((0,), (0,)), ((), ())), preferred_element_type=F32
    )
    factor = jnp.where(last_start < first, jnp.exp(ending), 0.0)
    factor = spread(jnp.broadcast_to(factor, (8, 128)))
    inside_ref[0] = running[...]
    gain_ref[0] = gains[...]
    running[...] = factor[0:1, :] * running[...] + local_state
    gains[...] = gains[...] * factor

    @pl.when(block == pl.num_programs(0) - 1)
    def _():
        packed_ref[0:STATE, :] = running[...].astype(BF16)
        high = gains[...].astype(BF16)
        low = (gains[...] - high.astype(F32)).astype(BF16)
        packed_ref[STATE : STATE + 16, :] = jnp.concatenate([high, low], axis=0)


def block_kernel(
    starts, base, act_ref, cum_ref, step_ref, inside_ref, gain_ref, y_ref, reach_ref
):
    first = base[0] + pl.program_id(0) * BLOCK
    act = act_ref[...]
    x_act, b_act, c_act = act[:, 0:256], act[:, 256:384], act[:, 384:512]
    cumulative = cum_ref[...]
    cum_rows, step_rows = cumulative.T, step_ref[...].T
    products = lax.dot_general(
        c_act, b_act, (((1,), (1,)), ((), ())), preferred_element_type=F32
    )
    start = doc_start(starts, first + lax.broadcasted_iota(jnp.int32, (BLOCK, 128), 0))
    row = lax.broadcasted_iota(jnp.int32, (BLOCK, BLOCK), 0)
    column = lax.broadcasted_iota(jnp.int32, (BLOCK, BLOCK), 1)
    allowed = (column <= row) & (first + column >= start[:, 0:1])
    parts = []
    for h in range(4):
        gap = cumulative[:, h : h + 1] - cum_rows[h : h + 1, :]
        decay = jnp.exp(jnp.where(allowed, gap, FAR))
        scores = (products * decay * step_rows[h : h + 1, :]).astype(BF16)
        parts.append(
            jnp.dot(scores, x_act[:, h * WIDTH : (h + 1) * WIDTH], preferred_element_type=F32)
        )
    y_inner = jnp.concatenate(parts, axis=1)
    reach = spread(jnp.where(start < first, jnp.exp(cumulative), 0.0))
    inside = inside_ref[0]
    high = inside.astype(BF16)
    low = (inside - high.astype(F32)).astype(BF16)
    carried = jnp.dot(c_act, high, preferred_element_type=F32) + jnp.dot(
        c_act, low, preferred_element_type=F32
    )
    y_ref[...] = y_inner + reach * carried + x_act.astype(F32)
    reach_ref[...] = reach * gain_ref[0, 0:1, :]


def gain_of(packed):
    return packed[STATE : STATE + 8].astype(F32) + packed[STATE + 8 : STATE + 16].astype(F32)


def carry_kernel(own_ref, before_ref, out_ref):
    own, before = own_ref[...], before_ref[...]
    total = own[0:STATE].astype(F32) + gain_of(own)[0:1] * before[0:STATE].astype(F32)
    out_ref[0:STATE, :] = total.astype(BF16)
    out_ref[STATE : STATE + 16, :] = own[STATE : STATE + 16]


def finish_kernel(
    scalars, before_ref, shards_ref, act_ref, y_ref, reach_ref, tok_ref, w_ref, out_ref,
    total, weights,
):
    step = pl.program_id(0)

    @pl.when(step == 0)
    def _():
        for k in range(Z):
            for slot in range(YH):
                row = ((scalars[2] + slot) % YH * Z + k) * 256
                weights[pl.ds(pl.multiple_of(row, 256), 256), :] = w_ref[k, slot]

    part = jnp.dot(
        tok_ref[...],
        weights[pl.ds(pl.multiple_of(step * CHUNK, CHUNK), CHUNK), :],
        preferred_element_type=F32,
    )

    @pl.when(step == 0)
    def _():
        total[...] = part

    @pl.when(step > 0)
    def _():
        total[...] += part

    @pl.when(step == pl.num_programs(0) - 1)
    def _():
        z = scalars[0]
        state = jnp.zeros((STATE, 256), F32)
        for k in range(Z - 1):
            piece = shards_ref[k]
            later = gain_of(piece)[0:1] * state + piece[0:STATE].astype(F32)
            state = jnp.where(k < z, later, state)
        entering = (state + before_ref[0:STATE, :].astype(F32)).astype(BF16)
        carried = jnp.dot(act_ref[...], entering, preferred_element_type=F32)
        gate = total[...].astype(BF16).astype(F32)
        out_ref[...] = ((y_ref[...] + reach_ref[...] * carried) * jax.nn.silu(gate)).astype(BF16)


def shape(dims, dtype):
    return jax.ShapeDtypeStruct(dims, dtype)


def work(flops, moved, exps=0):
    return pl.CostEstimate(flops=flops, bytes_accessed=moved, transcendentals=exps)


def run_first(gathered, pieces, swapped, scalars):
    rows, depth = gathered.shape
    layout = tuple((offset, first, piece.shape[0]) for offset, first, piece in pieces)
    arrays = [in_hbm(piece) for _, _, piece in pieces] + [in_hbm(swapped)]
    last = rows // BLOCK - 1
    return call(
        functools.partial(first_kernel, layout),
        (1,),
        [pl.BlockSpec((BLOCK, depth), lambda *_: (last, 0))] + [whole(a.shape) for a in arrays],
        [pl.BlockSpec((BLOCK, 640), lambda *_: (last, 0)), held(None)],
        [shape((rows, 640), BF16), shape((depth, 640), BF16)],
        prefetch=1,
        cost=work(2 * BLOCK * depth * 640, 12 << 20),
        room=24,
    )(scalars, gathered, *arrays)


def run_rest(gathered, weights, proj):
    rows, depth = gathered.shape
    count = rows - BLOCK
    return call(
        rest_kernel,
        (depth // CHUNK,),
        [
            pl.BlockSpec((count, CHUNK), lambda k: (0, k)),
            held(weights),
            pl.BlockSpec(memory_space=pl.ANY),
        ],
        pl.BlockSpec((count, 640), lambda k: (0, 0)),
        shape((rows, 640), BF16),
        scratch=[pltpu.VMEM((count, 640), F32)],
        cost=work(2 * count * depth * 640, 8 << 20),
        room=16,
        aliases={2: 0},
    )(gathered, weights, proj)


def run_state(starts, base, proj, rim, taps, small):
    rows = proj.shape[0]
    blocks = rows // BLOCK
    return call(
        state_kernel,
        (blocks,),
        [rows_of((BLOCK, 640)), whole((8, 512)), whole((4, 512)), whole((8, 128))],
        [
            rows_of((BLOCK, 512)),
            rows_of((BLOCK, 128)),
            rows_of((BLOCK, 128)),
            rows_of((1, STATE, 256)),
            rows_of((1, 8, 256)),
            whole((STATE + 16, 256)),
        ],
        [
            shape((rows, 512), BF16),
            shape((rows, 128), F32),
            shape((rows, 128), F32),
            shape((blocks, STATE, 256), F32),
            shape((blocks, 8, 256), F32),
            shape((STATE + 16, 256), BF16),
        ],
        scratch=[
            pltpu.VMEM((8 + BLOCK, 512), F32),
            pltpu.VMEM((STATE, 256), F32),
            pltpu.VMEM((8, 256), F32),
        ],
        prefetch=2,
        cost=work(2 * rows * 128 * 256, 4 << 20, rows * 1024),
    )(starts, base, proj, rim, taps, small)


def run_blocks(starts, base, act, cum, step, inside, gains):
    rows = act.shape[0]
    blocks = rows // BLOCK
    return call(
        block_kernel,
        (blocks,),
        [
            rows_of((BLOCK, 512)),
            rows_of((BLOCK, 128)),
            rows_of((BLOCK, 128)),
            rows_of((1, STATE, 256)),
            rows_of((1, 8, 256)),
        ],
        [rows_of((BLOCK, 256)), rows_of((BLOCK, 256))],
        [pltpu.HBM((rows, 256), F32), pltpu.HBM((rows, 256), F32)],
        prefetch=2,
        cost=work(2 * rows * 256 * 1024, 5 << 20, rows * 1280),
    )(starts, base, act, cum, step, inside, gains)


def run_carry(own, before):
    return call(
        carry_kernel,
        (1,),
        [held(own), held(before)],
        held(own),
        shape(own.shape, BF16),
        cost=work(1 << 17, 1 << 18),
        room=4,
    )(own, before)


def run_finish(scalars, before, shards, act, y, reach, gathered, gate_all):
    rows, depth = gathered.shape
    return call(
        finish_kernel,
        (depth // CHUNK,),
        [
            held(before),
            held(shards),
            pl.BlockSpec((rows, 128), lambda *_: (0, 3)),
            whole((rows, 256)),
            whole((rows, 256)),
            pl.BlockSpec((rows, CHUNK), lambda k, *_: (0, k)),
            whole(gate_all.shape),
        ],
        whole((rows, 256)),
        shape((rows, 256), BF16),
        scratch=[pltpu.VMEM((rows, 256), F32), pltpu.VMEM((depth, 256), BF16)],
        prefetch=1,
        cost=work(2 * rows * (128 + depth) * 256, 13 << 20),
        room=28,
    )(scalars, before, shards, act, y, reach, gathered, gate_all)


def local(
    tokens,
    doc_lengths,
    value_weight,
    gate_weight,
    state_weight,
    step_weight,
    value_conv,
    state_conv,
    step_bias,
    log_rate,
):
    tok_dev = tokens.shape[0] * X * Y * C
    heads_here = step_weight.shape[1]
    core = lax.axis_index("c")
    z = lax.axis_index("z")
    group = lax.axis_index("x") * 2 + lax.axis_index("y") // 2
    gathered = lax.all_gather(tokens, HEAD, axis=0, tiled=True)

    state_half = lax.dynamic_slice(state_weight, (group, core * 128, 0), (1, 128, 256))[0]
    conv_own = lax.dynamic_index_in_dim(state_conv, group, 0, keepdims=False)
    step_rows = jnp.pad(step_weight.T, ((0, 8 - heads_here), (0, 0)))
    pack = jnp.concatenate([value_weight, state_half, step_rows], axis=0)
    both = lax.all_gather(pack, "yh", axis=0, tiled=False)
    pieces = ring_gather(both)
    gate_own, _ = lax.optimization_barrier((gate_weight, pieces[2][2]))
    gate_far = lax.ppermute(gate_own, "yh", ring(YH, 1))
    halves = jnp.concatenate([piece[:, 256:384] for _, _, piece in pieces], axis=0)
    halves = lax.ppermute(halves, "c", [(0, 1), (1, 0)])
    scalars = jnp.stack([z, core, lax.axis_index("yh")]).astype(jnp.int32)
    gate_part = jnp.stack([gate_own, gate_far])
    gate_part, gathered, halves = lax.optimization_barrier((gate_part, gathered, halves))
    gate_all = lax.all_gather(gate_part, "z", axis=0, tiled=False)
    gathered = in_hbm(gathered)
    proj, weights = run_first(gathered, pieces, halves, scalars)
    rim = along_seq(proj[-8:, :512], 1)
    proj = run_rest(gathered, weights, proj)

    starts = (jnp.cumsum(doc_lengths) - doc_lengths).astype(jnp.int32)
    base = (lax.axis_index(SEQ) * tok_dev).astype(jnp.int32).reshape(1)
    taps = jnp.concatenate([value_conv, conv_own], axis=1)
    small = jnp.pad(jnp.stack([step_bias, log_rate]), ((0, 6), (0, 128 - heads_here)))
    act, cum, step, inside, gains, packed = run_state(starts, base, proj, rim, taps, small)
    before = lax.ppermute(packed, SEQ, [(Z - 1, Z)])
    y, reach = run_blocks(starts, base, act, cum, step, inside, gains)
    carried = run_carry(packed, before)
    shards = lax.all_gather(carried, "z", axis=0, tiled=False)
    return run_finish(
        scalars, before, shards, act, in_hbm(y), in_hbm(reach), gathered, in_hbm(gate_all)
    )


def solution(mesh):
    grid = Mesh(mesh.devices.reshape(YH, Z, X, Y, C), SEQ + HEAD)
    return jax.shard_map(
        local,
        mesh=grid,
        in_specs=(
            P(SEQ + HEAD, None),
            P(),
            P(SEQ, HEAD),
            P(SEQ, HEAD),
            P(None, SEQ, None),
            P(SEQ, HEAD),
            P(None, HEAD),
            P(),
            P(HEAD),
            P(HEAD),
        ),
        out_specs=P(SEQ, HEAD),
        check_vma=False,
    )
```

```python
import functools

import jax
import jax.numpy as jnp
from jax import lax
from jax.experimental import pallas as pl
from jax.experimental.pallas import tpu as pltpu
from jax.sharding import Mesh
from jax.sharding import PartitionSpec as P

HEADS = 128
GROUPS = 8
BLOCK = 256
STATE = 128
WIDTH = 64
YH, Z, X, Y, C = 2, 8, 4, 4, 2
SEQ = ("yh", "z")
HEAD = ("x", "y", "c")
F32 = jnp.float32
BF16 = jnp.bfloat16
MIB = 1024 * 1024
FAR = -1e30
TALL = 512


def ring(count, step):
    return [(i, (i + step) % count) for i in range(count)]


def along_seq(value, step):
    return lax.ppermute(value, SEQ, [(i, i + step) for i in range(YH * Z - step)])


def ring_gather(block, gate):
    pieces = [(0, 0, block)]
    right = left = block
    for step in range(1, 4):
        if step == 3:
            left, far = lax.optimization_barrier((left, far))
        right = lax.ppermute(right, "z", ring(Z, 1))
        left = lax.ppermute(left, "z", ring(Z, -1))
        pieces += [(Z - step, 0, right), (step, 0, left)]
        if step == 1:
            gate, right = lax.optimization_barrier((gate, right))
            far = lax.ppermute(gate, "yh", ring(YH, 1))
    right = lax.ppermute(right[:1], "z", ring(Z, 1))
    left = lax.ppermute(left[1:], "z", ring(Z, -1))
    return pieces + [(4, 0, right), (4, 1, left)], far


def call(
    kernel, grid, in_specs, out_specs, out_shape, scratch=(), prefetch=0, cost=None, room=12,
    aliases=None,
):
    return pl.pallas_call(
        kernel,
        grid_spec=pltpu.PrefetchScalarGridSpec(
            num_scalar_prefetch=prefetch,
            grid=grid,
            in_specs=in_specs,
            out_specs=out_specs,
            scratch_shapes=scratch,
        ),
        out_shape=out_shape,
        input_output_aliases=aliases or {},
        compiler_params=pltpu.CompilerParams(
            vmem_limit_bytes=room * MIB, dimension_semantics=("arbitrary",) * len(grid)
        ),
        cost_estimate=cost,
    )


def whole(shape):
    return pl.BlockSpec(shape, lambda *_: (0,) * len(shape))


def in_hbm(value):
    return pltpu.with_memory_space_constraint(value, pltpu.HBM)


def held(_):
    return pl.BlockSpec(memory_space=pltpu.VMEM)


def rows_of(shape):
    return pl.BlockSpec(shape, lambda i, *_: (i,) + (0,) * (len(shape) - 1))


def first_kernel(layout, scalars, tok_ref, *refs):
    pieces, other, proj_ref, out = refs[:-3], refs[-3], refs[-2], refs[-1]
    z, core = scalars[0], scalars[1]
    count = 0
    for (offset, first, yh_count), piece in zip(layout, pieces):
        source = lax.rem(z + offset, Z)
        for local_yh in range(yh_count):
            start = pl.multiple_of(((first + local_yh) * Z + source) * 256, 256)
            out[pl.ds(start, 256), 0:256] = piece[local_yh, 0:256, :]
            own = pl.multiple_of(start + core * 128, 128)
            its = pl.multiple_of(start + (1 - core) * 128, 128)
            out[pl.ds(own, 128), 256:512] = piece[local_yh, 256:384, :]
            out[pl.ds(its, 128), 256:512] = other[count, :, :]
            count += 1
            steps = piece[local_yh, 384:392, :].astype(F32).T
            steps = jnp.concatenate([steps, jnp.zeros((256, 120), F32)], axis=1)
            out[pl.ds(start, 256), 512:640] = steps.astype(BF16)
    project(tok_ref, out, proj_ref)


def project(tok_ref, w_ref, out_ref):
    out_ref[...] = jnp.dot(
        tok_ref[...], w_ref[...], preferred_element_type=F32
    ).astype(BF16)


def rest_kernel(tok_ref, w_ref, _, out_ref):
    project(tok_ref, w_ref, out_ref)


def spread(columns):
    rows = columns.shape[0]
    lane = lax.broadcasted_iota(jnp.int32, (rows, 128), 1)
    wide = [jnp.broadcast_to(columns[:, h : h + 1], (rows, 128)) for h in range(4)]
    return jnp.concatenate(
        [jnp.where(lane < WIDTH, wide[0], wide[1]), jnp.where(lane < WIDTH, wide[2], wide[3])],
        axis=1,
    )


def doc_start(starts, positions):
    found = jnp.zeros(positions.shape, jnp.int32)
    for j in range(16):
        found = jnp.where(starts[j] <= positions, starts[j], found)
    return found


def state_kernel(
    starts, base, proj_ref, rim_ref, taps_ref, small_ref,
    act_ref, cum_ref, step_ref, inside_ref, gain_ref, packed_ref,
    ext, running, gains,
):
    block = pl.program_id(0)
    first = base[0] + block * BLOCK

    @pl.when(block == 0)
    def _():
        ext[0:8, :] = rim_ref[...].astype(F32)
        running[...] = jnp.zeros_like(running)
        gains[...] = jnp.ones_like(gains)

    proj = proj_ref[...]
    tile = proj[:, 0:512].astype(F32)
    ext[8 : 8 + BLOCK, :] = tile
    positions = first + lax.broadcasted_iota(jnp.int32, (BLOCK, 128), 0)
    start = doc_start(starts, positions)
    depth = (positions - start)[:, 0:1]
    summed = taps_ref[3:4, :] * tile
    for lag in (1, 2, 3):
        window = ext[8 - lag : 8 - lag + BLOCK, :]
        summed = summed + jnp.where(depth >= lag, taps_ref[3 - lag : 4 - lag, :] * window, 0.0)
    act = jax.nn.silu(summed).astype(BF16)
    act_ref[...] = act
    ext[0:8, :] = tile[BLOCK - 8 :, :]

    step = jax.nn.softplus(proj[:, 512:640].astype(F32) + small_ref[0:1, :])
    decay = -jnp.exp(small_ref[1:2, :]) * step
    tri = (
        lax.broadcasted_iota(jnp.int32, (BLOCK, BLOCK), 1)
        <= lax.broadcasted_iota(jnp.int32, (BLOCK, BLOCK), 0)
    ).astype(F32)
    cumulative = jnp.dot(
        tri, decay, preferred_element_type=F32, precision=lax.Precision.HIGHEST
    )
    cum_ref[...] = cumulative
    step_ref[...] = step
    ending = cumulative[BLOCK - 1 : BLOCK, :]
    last_start = start[BLOCK - 1 : BLOCK, :]
    trailing = jnp.where(positions >= last_start, jnp.exp(ending - cumulative) * step, 0.0)
    weighted = (spread(trailing) * act[:, 0:256].astype(F32)).astype(BF16)
    local_state = lax.dot_general(
        act[:, 256:384], weighted, (((0,), (0,)), ((), ())), preferred_element_type=F32
    )
    factor = jnp.where(last_start < first, jnp.exp(ending), 0.0)
    factor = spread(jnp.broadcast_to(factor, (8, 128)))
    inside_ref[0] = running[...]
    gain_ref[0] = gains[...]
    running[...] = factor[0:1, :] * running[...] + local_state
    gains[...] = gains[...] * factor

    @pl.when(block == pl.num_programs(0) - 1)
    def _():
        packed_ref[0:STATE, :] = running[...].astype(BF16)
        high = gains[...].astype(BF16)
        low = (gains[...] - high.astype(F32)).astype(BF16)
        packed_ref[STATE : STATE + 16, :] = jnp.concatenate([high, low], axis=0)


def block_kernel(
    starts, base, act_ref, cum_ref, step_ref, inside_ref, gain_ref, y_ref, reach_ref
):
    first = base[0] + pl.program_id(0) * BLOCK
    act = act_ref[...]
    x_act, b_act, c_act = act[:, 0:256], act[:, 256:384], act[:, 384:512]
    cumulative = cum_ref[...]
    cum_rows, step_rows = cumulative.T, step_ref[...].T
    products = lax.dot_general(
        c_act, b_act, (((1,), (1,)), ((), ())), preferred_element_type=F32
    )
    start = doc_start(starts, first + lax.broadcasted_iota(jnp.int32, (BLOCK, 128), 0))
    row = lax.broadcasted_iota(jnp.int32, (BLOCK, BLOCK), 0)
    column = lax.broadcasted_iota(jnp.int32, (BLOCK, BLOCK), 1)
    allowed = (column <= row) & (first + column >= start[:, 0:1])
    parts = []
    for h in range(4):
        gap = cumulative[:, h : h + 1] - cum_rows[h : h + 1, :]
        decay = jnp.exp(jnp.where(allowed, gap, FAR))
        scores = (products * decay * step_rows[h : h + 1, :]).astype(BF16)
        parts.append(
            jnp.dot(scores, x_act[:, h * WIDTH : (h + 1) * WIDTH], preferred_element_type=F32)
        )
    y_inner = jnp.concatenate(parts, axis=1)
    reach = spread(jnp.where(start < first, jnp.exp(cumulative), 0.0))
    inside = inside_ref[0]
    high = inside.astype(BF16)
    low = (inside - high.astype(F32)).astype(BF16)
    carried = jnp.dot(c_act, high, preferred_element_type=F32) + jnp.dot(
        c_act, low, preferred_element_type=F32
    )
    y_ref[...] = y_inner + reach * carried + x_act.astype(F32)
    reach_ref[...] = reach * gain_ref[0, 0:1, :]


def gain_of(packed):
    return packed[STATE : STATE + 8].astype(F32) + packed[STATE + 8 : STATE + 16].astype(F32)


def carry_kernel(own_ref, before_ref, out_ref):
    own, before = own_ref[...], before_ref[...]
    total = own[0:STATE].astype(F32) + gain_of(own)[0:1] * before[0:STATE].astype(F32)
    out_ref[0:STATE, :] = total.astype(BF16)
    out_ref[STATE : STATE + 16, :] = own[STATE : STATE + 16]


def finish_kernel(
    scalars, before_ref, shards_ref, act_ref, y_ref, reach_ref, tok_ref, w_ref, out_ref,
    entering, weights,
):
    @pl.when(pl.program_id(0) == 0)
    def _():
        z = scalars[0]
        state = jnp.zeros((STATE, 256), F32)
        for k in range(Z - 1):
            piece = shards_ref[k]
            later = gain_of(piece)[0:1] * state + piece[0:STATE].astype(F32)
            state = jnp.where(k < z, later, state)
        entering[...] = (state + before_ref[0:STATE, :].astype(F32)).astype(BF16)
        for k in range(Z):
            for slot in range(YH):
                row = ((scalars[2] + slot) % YH * Z + k) * 256
                weights[pl.ds(pl.multiple_of(row, 256), 256), :] = w_ref[k, slot]

    gate = jnp.dot(tok_ref[...], weights[...], preferred_element_type=F32).astype(BF16)
    carried = jnp.dot(act_ref[...], entering[...], preferred_element_type=F32)
    total = y_ref[...] + reach_ref[...] * carried
    out_ref[...] = (total * jax.nn.silu(gate.astype(F32))).astype(BF16)


def shape(dims, dtype):
    return jax.ShapeDtypeStruct(dims, dtype)


def work(flops, moved, exps=0):
    return pl.CostEstimate(flops=flops, bytes_accessed=moved, transcendentals=exps)


def run_first(gathered, pieces, swapped, scalars):
    rows, depth = gathered.shape
    layout = tuple((offset, first, piece.shape[0]) for offset, first, piece in pieces)
    arrays = [in_hbm(piece) for _, _, piece in pieces] + [in_hbm(swapped)]
    last = rows // BLOCK - 1
    return call(
        functools.partial(first_kernel, layout),
        (1,),
        [pl.BlockSpec((BLOCK, depth), lambda *_: (last, 0))] + [whole(a.shape) for a in arrays],
        [pl.BlockSpec((BLOCK, 640), lambda *_: (last, 0)), held(None)],
        [shape((rows, 640), BF16), shape((depth, 640), BF16)],
        prefetch=1,
        cost=work(2 * BLOCK * depth * 640, 12 << 20),
        room=24,
    )(scalars, gathered, *arrays)


def run_rest(gathered, weights, proj):
    rows, depth = gathered.shape
    tile = (rows - BLOCK) // 2
    return call(
        rest_kernel,
        (2,),
        [rows_of((tile, depth)), held(weights), pl.BlockSpec(memory_space=pl.ANY)],
        rows_of((tile, 640)),
        shape((rows, 640), BF16),
        cost=work(2 * (rows - BLOCK) * depth * 640, 8 << 20),
        room=20,
        aliases={2: 0},
    )(gathered, weights, proj)


def run_state(starts, base, proj, rim, taps, small):
    rows = proj.shape[0]
    blocks = rows // BLOCK
    return call(
        state_kernel,
        (blocks,),
        [rows_of((BLOCK, 640)), whole((8, 512)), whole((4, 512)), whole((8, 128))],
        [
            rows_of((BLOCK, 512)),
            rows_of((BLOCK, 128)),
            rows_of((BLOCK, 128)),
            rows_of((1, STATE, 256)),
            rows_of((1, 8, 256)),
            whole((STATE + 16, 256)),
        ],
        [
            shape((rows, 512), BF16),
            shape((rows, 128), F32),
            shape((rows, 128), F32),
            shape((blocks, STATE, 256), F32),
            shape((blocks, 8, 256), F32),
            shape((STATE + 16, 256), BF16),
        ],
        scratch=[
            pltpu.VMEM((8 + BLOCK, 512), F32),
            pltpu.VMEM((STATE, 256), F32),
            pltpu.VMEM((8, 256), F32),
        ],
        prefetch=2,
        cost=work(2 * rows * 128 * 256, 4 << 20, rows * 1024),
    )(starts, base, proj, rim, taps, small)


def run_blocks(starts, base, act, cum, step, inside, gains):
    rows = act.shape[0]
    blocks = rows // BLOCK
    return call(
        block_kernel,
        (blocks,),
        [
            rows_of((BLOCK, 512)),
            rows_of((BLOCK, 128)),
            rows_of((BLOCK, 128)),
            rows_of((1, STATE, 256)),
            rows_of((1, 8, 256)),
        ],
        [rows_of((BLOCK, 256)), rows_of((BLOCK, 256))],
        [pltpu.HBM((rows, 256), F32), pltpu.HBM((rows, 256), F32)],
        prefetch=2,
        cost=work(2 * rows * 256 * 1024, 5 << 20, rows * 1280),
    )(starts, base, act, cum, step, inside, gains)


def run_carry(own, before):
    return call(
        carry_kernel,
        (1,),
        [held(own), held(before)],
        held(own),
        shape(own.shape, BF16),
        cost=work(1 << 17, 1 << 18),
        room=4,
    )(own, before)


def run_finish(scalars, before, shards, act, y, reach, gathered, gate_all):
    rows, depth = gathered.shape
    return call(
        finish_kernel,
        (rows // TALL,),
        [
            held(before),
            held(shards),
            pl.BlockSpec((TALL, 128), lambda i, *_: (i, 3)),
            rows_of((TALL, 256)),
            rows_of((TALL, 256)),
            rows_of((TALL, depth)),
            whole(gate_all.shape),
        ],
        rows_of((TALL, 256)),
        shape((rows, 256), BF16),
        scratch=[pltpu.VMEM((STATE, 256), BF16), pltpu.VMEM((depth, 256), BF16)],
        prefetch=1,
        cost=work(2 * rows * (128 + depth) * 256, 13 << 20),
        room=28,
    )(scalars, before, shards, act, y, reach, gathered, gate_all)


def local(
    tokens,
    doc_lengths,
    value_weight,
    gate_weight,
    state_weight,
    step_weight,
    value_conv,
    state_conv,
    step_bias,
    log_rate,
):
    tok_dev = tokens.shape[0] * X * Y * C
    heads_here = step_weight.shape[1]
    core = lax.axis_index("c")
    z = lax.axis_index("z")
    group = lax.axis_index("x") * 2 + lax.axis_index("y") // 2
    gathered = lax.all_gather(tokens, HEAD, axis=0, tiled=True)

    state_half = lax.dynamic_slice(state_weight, (group, core * 128, 0), (1, 128, 256))[0]
    conv_own = lax.dynamic_index_in_dim(state_conv, group, 0, keepdims=False)
    step_rows = jnp.pad(step_weight.T, ((0, 8 - heads_here), (0, 0)))
    pack = jnp.concatenate([value_weight, state_half, step_rows], axis=0)
    both = lax.all_gather(pack, "yh", axis=0, tiled=False)
    pieces, gate_far = ring_gather(both, gate_weight)
    halves = jnp.concatenate([piece[:, 256:384] for _, _, piece in pieces], axis=0)
    halves = lax.ppermute(halves, "c", [(0, 1), (1, 0)])
    scalars = jnp.stack([z, core, lax.axis_index("yh")]).astype(jnp.int32)
    gate_part = jnp.stack([gate_weight, gate_far])
    gate_part, gathered, halves = lax.optimization_barrier((gate_part, gathered, halves))
    gate_all = lax.all_gather(gate_part, "z", axis=0, tiled=False)
    gathered = in_hbm(gathered)
    proj, weights = run_first(gathered, pieces, halves, scalars)
    rim = along_seq(proj[-8:, :512], 1)
    proj = run_rest(gathered, weights, proj)

    starts = (jnp.cumsum(doc_lengths) - doc_lengths).astype(jnp.int32)
    base = (lax.axis_index(SEQ) * tok_dev).astype(jnp.int32).reshape(1)
    taps = jnp.concatenate([value_conv, conv_own], axis=1)
    small = jnp.pad(jnp.stack([step_bias, log_rate]), ((0, 6), (0, 128 - heads_here)))
    act, cum, step, inside, gains, packed = run_state(starts, base, proj, rim, taps, small)
    before = lax.ppermute(packed, SEQ, [(Z - 1, Z)])
    y, reach = run_blocks(starts, base, act, cum, step, inside, gains)
    carried = run_carry(packed, before)
    shards = lax.all_gather(carried, "z", axis=0, tiled=False)
    return run_finish(
        scalars, before, shards, act, in_hbm(y), in_hbm(reach), gathered, in_hbm(gate_all)
    )


def solution(mesh):
    grid = Mesh(mesh.devices.reshape(YH, Z, X, Y, C), SEQ + HEAD)
    return jax.shard_map(
        local,
        mesh=grid,
        in_specs=(
            P(SEQ + HEAD, None),
            P(),
            P(SEQ, HEAD),
            P(SEQ, HEAD),
            P(None, SEQ, None),
            P(SEQ, HEAD),
            P(None, HEAD),
            P(),
            P(HEAD),
            P(HEAD),
        ),
        out_specs=P(SEQ, HEAD),
        check_vma=False,
    )
```

```python
import functools

import jax
import jax.numpy as jnp
from jax import lax
from jax.experimental import pallas as pl
from jax.experimental.pallas import tpu as pltpu
from jax.sharding import Mesh
from jax.sharding import PartitionSpec as P

HEADS = 128
GROUPS = 8
BLOCK = 256
STATE = 128
WIDTH = 64
YH, Z, X, Y, C = 2, 8, 4, 4, 2
PAIRS = Z // 2
RING = ("zh", "zc")
SEQ = ("yh",) + RING
HEAD = ("x", "y", "c")
F32 = jnp.float32
BF16 = jnp.bfloat16
MIB = 1024 * 1024
FAR = -1e30
TALL = 512


def ring(count, step):
    return [(i, (i + step) % count) for i in range(count)]


def along_seq(value, step):
    return lax.ppermute(value, SEQ, [(i, i + step) for i in range(YH * Z - step)])


def ring_gather(block):
    pieces = [(0, 0, block)]
    right = left = block
    for step in range(1, 4):
        right = lax.ppermute(right, RING, ring(Z, 1))
        left = lax.ppermute(left, RING, ring(Z, -1))
        pieces += [(Z - step, 0, right), (step, 0, left)]
    right = lax.ppermute(right[:1], RING, ring(Z, 1))
    left = lax.ppermute(left[1:], RING, ring(Z, -1))
    return pieces + [(4, 0, right), (4, 1, left)]


def call(
    kernel, grid, in_specs, out_specs, out_shape, scratch=(), prefetch=0, cost=None, room=12,
    aliases=None,
):
    return pl.pallas_call(
        kernel,
        grid_spec=pltpu.PrefetchScalarGridSpec(
            num_scalar_prefetch=prefetch,
            grid=grid,
            in_specs=in_specs,
            out_specs=out_specs,
            scratch_shapes=scratch,
        ),
        out_shape=out_shape,
        input_output_aliases=aliases or {},
        compiler_params=pltpu.CompilerParams(
            vmem_limit_bytes=room * MIB, dimension_semantics=("arbitrary",) * len(grid)
        ),
        cost_estimate=cost,
    )


def whole(shape):
    return pl.BlockSpec(shape, lambda *_: (0,) * len(shape))


def in_hbm(value):
    return pltpu.with_memory_space_constraint(value, pltpu.HBM)


def held(_):
    return pl.BlockSpec(memory_space=pltpu.VMEM)


def rows_of(shape):
    return pl.BlockSpec(shape, lambda i, *_: (i,) + (0,) * (len(shape) - 1))


def first_kernel(layout, scalars, tok_ref, *refs):
    pieces, other, proj_ref, out = refs[:-3], refs[-3], refs[-2], refs[-1]
    z, core = scalars[0], scalars[1]
    count = 0
    for (offset, first, yh_count), piece in zip(layout, pieces):
        source = lax.rem(z + offset, Z)
        for local_yh in range(yh_count):
            start = pl.multiple_of(((first + local_yh) * Z + source) * 256, 256)
            out[pl.ds(start, 256), 0:256] = piece[local_yh, 0:256, :]
            own = pl.multiple_of(start + core * 128, 128)
            its = pl.multiple_of(start + (1 - core) * 128, 128)
            out[pl.ds(own, 128), 256:512] = piece[local_yh, 256:384, :]
            out[pl.ds(its, 128), 256:512] = other[count, :, :]
            count += 1
            steps = piece[local_yh, 384:392, :].astype(F32).T
            steps = jnp.concatenate([steps, jnp.zeros((256, 120), F32)], axis=1)
            out[pl.ds(start, 256), 512:640] = steps.astype(BF16)
    project(tok_ref, out, proj_ref)


def project(tok_ref, w_ref, out_ref):
    out_ref[...] = jnp.dot(
        tok_ref[...], w_ref[...], preferred_element_type=F32
    ).astype(BF16)


def rest_kernel(tok_ref, w_ref, _, out_ref):
    project(tok_ref, w_ref, out_ref)


def spread(columns):
    rows = columns.shape[0]
    lane = lax.broadcasted_iota(jnp.int32, (rows, 128), 1)
    wide = [jnp.broadcast_to(columns[:, h : h + 1], (rows, 128)) for h in range(4)]
    return jnp.concatenate(
        [jnp.where(lane < WIDTH, wide[0], wide[1]), jnp.where(lane < WIDTH, wide[2], wide[3])],
        axis=1,
    )


def doc_start(starts, positions):
    found = jnp.zeros(positions.shape, jnp.int32)
    for j in range(16):
        found = jnp.where(starts[j] <= positions, starts[j], found)
    return found


def state_kernel(
    starts, base, proj_ref, rim_ref, taps_ref, small_ref,
    act_ref, cum_ref, step_ref, inside_ref, gain_ref, packed_ref,
    ext, running, gains,
):
    block = pl.program_id(0)
    first = base[0] + block * BLOCK

    @pl.when(block == 0)
    def _():
        ext[0:8, :] = rim_ref[...].astype(F32)
        running[...] = jnp.zeros_like(running)
        gains[...] = jnp.ones_like(gains)

    proj = proj_ref[...]
    tile = proj[:, 0:512].astype(F32)
    ext[8 : 8 + BLOCK, :] = tile
    positions = first + lax.broadcasted_iota(jnp.int32, (BLOCK, 128), 0)
    start = doc_start(starts, positions)
    depth = (positions - start)[:, 0:1]
    summed = taps_ref[3:4, :] * tile
    for lag in (1, 2, 3):
        window = ext[8 - lag : 8 - lag + BLOCK, :]
        summed = summed + jnp.where(depth >= lag, taps_ref[3 - lag : 4 - lag, :] * window, 0.0)
    act = jax.nn.silu(summed).astype(BF16)
    act_ref[...] = act
    ext[0:8, :] = tile[BLOCK - 8 :, :]

    step = jax.nn.softplus(proj[:, 512:640].astype(F32) + small_ref[0:1, :])
    decay = -jnp.exp(small_ref[1:2, :]) * step
    tri = (
        lax.broadcasted_iota(jnp.int32, (BLOCK, BLOCK), 1)
        <= lax.broadcasted_iota(jnp.int32, (BLOCK, BLOCK), 0)
    ).astype(F32)
    cumulative = jnp.dot(
        tri, decay, preferred_element_type=F32, precision=lax.Precision.HIGHEST
    )
    cum_ref[...] = cumulative
    step_ref[...] = step
    ending = cumulative[BLOCK - 1 : BLOCK, :]
    last_start = start[BLOCK - 1 : BLOCK, :]
    trailing = jnp.where(positions >= last_start, jnp.exp(ending - cumulative) * step, 0.0)
    weighted = (spread(trailing) * act[:, 0:256].astype(F32)).astype(BF16)
    local_state = lax.dot_general(
        act[:, 256:384], weighted, (((0,), (0,)), ((), ())), preferred_element_type=F32
    )
    factor = jnp.where(last_start < first, jnp.exp(ending), 0.0)
    factor = spread(jnp.broadcast_to(factor, (8, 128)))
    inside_ref[0] = running[...]
    gain_ref[0] = gains[...]
    running[...] = factor[0:1, :] * running[...] + local_state
    gains[...] = gains[...] * factor

    @pl.when(block == pl.num_programs(0) - 1)
    def _():
        packed_ref[0:STATE, :] = running[...].astype(BF16)
        high = gains[...].astype(BF16)
        low = (gains[...] - high.astype(F32)).astype(BF16)
        packed_ref[STATE : STATE + 16, :] = jnp.concatenate([high, low], axis=0)


def block_kernel(
    starts, base, act_ref, cum_ref, step_ref, inside_ref, gain_ref, y_ref, reach_ref
):
    first = base[0] + pl.program_id(0) * BLOCK
    act = act_ref[...]
    x_act, b_act, c_act = act[:, 0:256], act[:, 256:384], act[:, 384:512]
    cumulative = cum_ref[...]
    cum_rows, step_rows = cumulative.T, step_ref[...].T
    products = lax.dot_general(
        c_act, b_act, (((1,), (1,)), ((), ())), preferred_element_type=F32
    )
    start = doc_start(starts, first + lax.broadcasted_iota(jnp.int32, (BLOCK, 128), 0))
    row = lax.broadcasted_iota(jnp.int32, (BLOCK, BLOCK), 0)
    column = lax.broadcasted_iota(jnp.int32, (BLOCK, BLOCK), 1)
    allowed = (column <= row) & (first + column >= start[:, 0:1])
    parts = []
    for h in range(4):
        gap = cumulative[:, h : h + 1] - cum_rows[h : h + 1, :]
        decay = jnp.exp(jnp.where(allowed, gap, FAR))
        scores = (products * decay * step_rows[h : h + 1, :]).astype(BF16)
        parts.append(
            jnp.dot(scores, x_act[:, h * WIDTH : (h + 1) * WIDTH], preferred_element_type=F32)
        )
    y_inner = jnp.concatenate(parts, axis=1)
    reach = spread(jnp.where(start < first, jnp.exp(cumulative), 0.0))
    inside = inside_ref[0]
    high = inside.astype(BF16)
    low = (inside - high.astype(F32)).astype(BF16)
    carried = jnp.dot(c_act, high, preferred_element_type=F32) + jnp.dot(
        c_act, low, preferred_element_type=F32
    )
    y_ref[...] = y_inner + reach * carried + x_act.astype(F32)
    reach_ref[...] = reach * gain_ref[0, 0:1, :]


def gain_of(packed):
    return packed[STATE : STATE + 8].astype(F32) + packed[STATE + 8 : STATE + 16].astype(F32)


def pair_kernel(pair_ref, eight_ref, nine_ref, out_ref):
    even, odd = pair_ref[0], pair_ref[1]
    before = eight_ref[0:STATE, :].astype(F32) + nine_ref[0:STATE, :].astype(F32)
    total = even[0:STATE].astype(F32) + gain_of(even)[0:1] * before
    total = odd[0:STATE].astype(F32) + gain_of(odd)[0:1] * total
    gain = gain_of(even) * gain_of(odd)
    high = gain.astype(BF16)
    low = (gain - high.astype(F32)).astype(BF16)
    out_ref[0:STATE, :] = total.astype(BF16)
    out_ref[STATE : STATE + 16, :] = jnp.concatenate([high, low], axis=0)


def finish_kernel(
    scalars, eight_ref, nine_ref, own_ref, pairs_ref, act_ref, y_ref, reach_ref, tok_ref, w_ref,
    out_ref, entering, weights,
):
    @pl.when(pl.program_id(0) == 0)
    def _():
        pair, odd = scalars[0] // 2, scalars[0] % 2
        state = eight_ref[0:STATE, :].astype(F32) + nine_ref[0:STATE, :].astype(F32)
        for k in range(PAIRS - 1):
            piece = pairs_ref[k]
            later = gain_of(piece)[0:1] * state + piece[0:STATE].astype(F32)
            state = jnp.where(k < pair, later, state)
        even = own_ref[0]
        later = gain_of(even)[0:1] * state + even[0:STATE].astype(F32)
        entering[...] = jnp.where(odd == 1, later, state).astype(BF16)
        for k in range(Z):
            for yh in range(YH):
                weights[pl.ds((yh * Z + k) * 256, 256), :] = w_ref[k, yh]

    gate = jnp.dot(tok_ref[...], weights[...], preferred_element_type=F32).astype(BF16)
    carried = jnp.dot(act_ref[...], entering[...], preferred_element_type=F32)
    total = y_ref[...] + reach_ref[...] * carried
    out_ref[...] = (total * jax.nn.silu(gate.astype(F32))).astype(BF16)


def shape(dims, dtype):
    return jax.ShapeDtypeStruct(dims, dtype)


def work(flops, moved, exps=0):
    return pl.CostEstimate(flops=flops, bytes_accessed=moved, transcendentals=exps)


def run_first(gathered, pieces, swapped, scalars):
    rows, depth = gathered.shape
    layout = tuple((offset, first, piece.shape[0]) for offset, first, piece in pieces)
    arrays = [in_hbm(piece) for _, _, piece in pieces] + [in_hbm(swapped)]
    last = rows // BLOCK - 1
    return call(
        functools.partial(first_kernel, layout),
        (1,),
        [pl.BlockSpec((BLOCK, depth), lambda *_: (last, 0))] + [whole(a.shape) for a in arrays],
        [pl.BlockSpec((BLOCK, 640), lambda *_: (last, 0)), held(None)],
        [shape((rows, 640), BF16), shape((depth, 640), BF16)],
        prefetch=1,
        cost=work(2 * BLOCK * depth * 640, 12 << 20),
        room=24,
    )(scalars, gathered, *arrays)


def run_rest(gathered, weights, proj):
    rows, depth = gathered.shape
    count = rows // BLOCK - 1
    return call(
        rest_kernel,
        (count,),
        [rows_of((BLOCK, depth)), held(weights), pl.BlockSpec(memory_space=pl.ANY)],
        rows_of((BLOCK, 640)),
        shape((rows, 640), BF16),
        cost=work(2 * count * BLOCK * depth * 640, 8 << 20),
        room=16,
        aliases={2: 0},
    )(gathered, weights, proj)


def run_state(starts, base, proj, rim, taps, small):
    rows = proj.shape[0]
    blocks = rows // BLOCK
    return call(
        state_kernel,
        (blocks,),
        [rows_of((BLOCK, 640)), whole((8, 512)), whole((4, 512)), whole((8, 128))],
        [
            rows_of((BLOCK, 512)),
            rows_of((BLOCK, 128)),
            rows_of((BLOCK, 128)),
            rows_of((1, STATE, 256)),
            rows_of((1, 8, 256)),
            whole((STATE + 16, 256)),
        ],
        [
            shape((rows, 512), BF16),
            shape((rows, 128), F32),
            shape((rows, 128), F32),
            shape((blocks, STATE, 256), F32),
            shape((blocks, 8, 256), F32),
            shape((STATE + 16, 256), BF16),
        ],
        scratch=[
            pltpu.VMEM((8 + BLOCK, 512), F32),
            pltpu.VMEM((STATE, 256), F32),
            pltpu.VMEM((8, 256), F32),
        ],
        prefetch=2,
        cost=work(2 * rows * 128 * 256, 4 << 20, rows * 1024),
    )(starts, base, proj, rim, taps, small)


def run_blocks(starts, base, act, cum, step, inside, gains):
    rows = act.shape[0]
    blocks = rows // BLOCK
    return call(
        block_kernel,
        (blocks,),
        [
            rows_of((BLOCK, 512)),
            rows_of((BLOCK, 128)),
            rows_of((BLOCK, 128)),
            rows_of((1, STATE, 256)),
            rows_of((1, 8, 256)),
        ],
        [rows_of((BLOCK, 256)), rows_of((BLOCK, 256))],
        [pltpu.HBM((rows, 256), F32), pltpu.HBM((rows, 256), F32)],
        prefetch=2,
        cost=work(2 * rows * 256 * 1024, 5 << 20, rows * 1280),
    )(starts, base, act, cum, step, inside, gains)


def run_pair(pair, eight, nine):
    return call(
        pair_kernel,
        (1,),
        [held(pair), held(eight), held(nine)],
        held(eight),
        shape(eight.shape, BF16),
        cost=work(1 << 17, 1 << 18),
        room=4,
    )(pair, eight, nine)


def run_finish(scalars, eight, nine, own, pairs, act, y, reach, gathered, gate_all):
    rows, depth = gathered.shape
    return call(
        finish_kernel,
        (rows // TALL,),
        [
            held(eight),
            held(nine),
            held(own),
            held(pairs),
            pl.BlockSpec((TALL, 128), lambda i, *_: (i, 3)),
            rows_of((TALL, 256)),
            rows_of((TALL, 256)),
            rows_of((TALL, depth)),
            whole(gate_all.shape),
        ],
        rows_of((TALL, 256)),
        shape((rows, 256), BF16),
        scratch=[pltpu.VMEM((STATE, 256), BF16), pltpu.VMEM((depth, 256), BF16)],
        prefetch=1,
        cost=work(2 * rows * (128 + depth) * 256, 13 << 20),
        room=28,
    )(scalars, eight, nine, own, pairs, act, y, reach, gathered, gate_all)


def local(
    tokens,
    doc_lengths,
    value_weight,
    gate_weight,
    state_weight,
    step_weight,
    value_conv,
    state_conv,
    step_bias,
    log_rate,
):
    tok_dev = tokens.shape[0] * X * Y * C
    heads_here = step_weight.shape[1]
    core = lax.axis_index("c")
    z = lax.axis_index(RING)
    group = lax.axis_index("x") * 2 + lax.axis_index("y") // 2
    gathered = lax.all_gather(tokens, HEAD, axis=0, tiled=True)

    state_half = lax.dynamic_slice(state_weight, (group, core * 128, 0), (1, 128, 256))[0]
    conv_own = lax.dynamic_index_in_dim(state_conv, group, 0, keepdims=False)
    step_rows = jnp.pad(step_weight.T, ((0, 8 - heads_here), (0, 0)))
    pack = jnp.concatenate([value_weight, state_half, step_rows, gate_weight], axis=0)
    both = lax.all_gather(pack, "yh", axis=0, tiled=False)
    pieces = ring_gather(both[:, :392])
    halves = jnp.concatenate([piece[:, 256:384] for _, _, piece in pieces], axis=0)
    halves = lax.ppermute(halves, "c", [(0, 1), (1, 0)])
    scalars = jnp.stack([z, core]).astype(jnp.int32)
    gate_part, gathered, halves = lax.optimization_barrier((both[:, 392:], gathered, halves))
    gate_all = lax.all_gather(gate_part, RING, axis=0, tiled=False)
    gathered = in_hbm(gathered)
    proj, weights = run_first(gathered, pieces, halves, scalars)
    rim = along_seq(proj[-8:, :512], 1)
    proj = run_rest(gathered, weights, proj)

    starts = (jnp.cumsum(doc_lengths) - doc_lengths).astype(jnp.int32)
    base = (lax.axis_index(SEQ) * tok_dev).astype(jnp.int32).reshape(1)
    taps = jnp.concatenate([value_conv, conv_own], axis=1)
    small = jnp.pad(jnp.stack([step_bias, log_rate]), ((0, 6), (0, 128 - heads_here)))
    act, cum, step, inside, gains, packed = run_state(starts, base, proj, rim, taps, small)
    eight = lax.ppermute(packed, SEQ, [(Z - 1, Z)])
    nine = lax.ppermute(packed, SEQ, [(Z - 1, Z + 1)])
    y, reach = run_blocks(starts, base, act, cum, step, inside, gains)
    packed, y, reach = lax.optimization_barrier((packed, y, reach))
    own = lax.all_gather(packed, "zc", axis=0, tiled=False)
    own, eight, nine = lax.optimization_barrier((own, eight, nine))
    pairs = lax.all_gather(run_pair(own, eight, nine), "zh", axis=0, tiled=False)
    return run_finish(
        scalars, eight, nine, own, pairs, act, in_hbm(y), in_hbm(reach), gathered, in_hbm(gate_all)
    )


def solution(mesh):
    grid = Mesh(mesh.devices.reshape(YH, PAIRS, 2, X, Y, C), SEQ + HEAD)
    return jax.shard_map(
        local,
        mesh=grid,
        in_specs=(
            P(SEQ + HEAD, None),
            P(),
            P(SEQ, HEAD),
            P(SEQ, HEAD),
            P(None, SEQ, None),
            P(SEQ, HEAD),
            P(None, HEAD),
            P(),
            P(HEAD),
            P(HEAD),
        ),
        out_specs=P(SEQ, HEAD),
        check_vma=False,
    )
```

```python
import functools

import jax
import jax.numpy as jnp
from jax import lax
from jax.experimental import pallas as pl
from jax.experimental.pallas import tpu as pltpu
from jax.sharding import Mesh
from jax.sharding import PartitionSpec as P

HEADS = 128
GROUPS = 8
BLOCK = 256
STATE = 128
WIDTH = 64
YH, Z, X, Y, C = 2, 8, 4, 4, 2
PAIRS = Z // 2
RING = ("zh", "zc")
SEQ = ("yh",) + RING
HEAD = ("x", "y", "c")
F32 = jnp.float32
BF16 = jnp.bfloat16
MIB = 1024 * 1024
FAR = -1e30
TALL = 512


def ring(count, step):
    return [(i, (i + step) % count) for i in range(count)]


def along_seq(value, step):
    return lax.ppermute(value, SEQ, [(i, i + step) for i in range(YH * Z - step)])


def ring_gather(block):
    pieces = [(0, 0, block)]
    right = left = block
    for step in range(1, 4):
        right = lax.ppermute(right, RING, ring(Z, 1))
        left = lax.ppermute(left, RING, ring(Z, -1))
        pieces += [(Z - step, 0, right), (step, 0, left)]
    right = lax.ppermute(right[:1], RING, ring(Z, 1))
    left = lax.ppermute(left[1:], RING, ring(Z, -1))
    return pieces + [(4, 0, right), (4, 1, left)]


def call(
    kernel, grid, in_specs, out_specs, out_shape, scratch=(), prefetch=0, cost=None, room=12,
    aliases=None,
):
    return pl.pallas_call(
        kernel,
        grid_spec=pltpu.PrefetchScalarGridSpec(
            num_scalar_prefetch=prefetch,
            grid=grid,
            in_specs=in_specs,
            out_specs=out_specs,
            scratch_shapes=scratch,
        ),
        out_shape=out_shape,
        input_output_aliases=aliases or {},
        compiler_params=pltpu.CompilerParams(
            vmem_limit_bytes=room * MIB, dimension_semantics=("arbitrary",) * len(grid)
        ),
        cost_estimate=cost,
    )


def whole(shape):
    return pl.BlockSpec(shape, lambda *_: (0,) * len(shape))


def in_hbm(value):
    return pltpu.with_memory_space_constraint(value, pltpu.HBM)


def held(_):
    return pl.BlockSpec(memory_space=pltpu.VMEM)


def rows_of(shape):
    return pl.BlockSpec(shape, lambda i, *_: (i,) + (0,) * (len(shape) - 1))


def first_kernel(layout, scalars, tok_ref, *refs):
    pieces, other, proj_ref, out = refs[:-3], refs[-3], refs[-2], refs[-1]
    z, core = scalars[0], scalars[1]
    count = 0
    for (offset, first, yh_count), piece in zip(layout, pieces):
        source = lax.rem(z + offset, Z)
        for local_yh in range(yh_count):
            start = pl.multiple_of(((first + local_yh) * Z + source) * 256, 256)
            out[pl.ds(start, 256), 0:256] = piece[local_yh, 0:256, :]
            own = pl.multiple_of(start + core * 128, 128)
            its = pl.multiple_of(start + (1 - core) * 128, 128)
            out[pl.ds(own, 128), 256:512] = piece[local_yh, 256:384, :]
            out[pl.ds(its, 128), 256:512] = other[count, :, :]
            count += 1
            steps = piece[local_yh, 384:392, :].astype(F32).T
            steps = jnp.concatenate([steps, jnp.zeros((256, 120), F32)], axis=1)
            out[pl.ds(start, 256), 512:640] = steps.astype(BF16)
    project(tok_ref, out, proj_ref)


def project(tok_ref, w_ref, out_ref):
    out_ref[...] = jnp.dot(
        tok_ref[...], w_ref[...], preferred_element_type=F32
    ).astype(BF16)


def rest_kernel(tok_ref, w_ref, _, out_ref):
    project(tok_ref, w_ref, out_ref)


def spread(columns):
    rows = columns.shape[0]
    lane = lax.broadcasted_iota(jnp.int32, (rows, 128), 1)
    wide = [jnp.broadcast_to(columns[:, h : h + 1], (rows, 128)) for h in range(4)]
    return jnp.concatenate(
        [jnp.where(lane < WIDTH, wide[0], wide[1]), jnp.where(lane < WIDTH, wide[2], wide[3])],
        axis=1,
    )


def doc_start(starts, positions):
    found = jnp.zeros(positions.shape, jnp.int32)
    for j in range(16):
        found = jnp.where(starts[j] <= positions, starts[j], found)
    return found


def state_kernel(
    starts, base, proj_ref, rim_ref, taps_ref, small_ref,
    act_ref, cum_ref, step_ref, inside_ref, gain_ref, packed_ref,
    ext, running, gains,
):
    block = pl.program_id(0)
    first = base[0] + block * BLOCK

    @pl.when(block == 0)
    def _():
        ext[0:8, :] = rim_ref[...].astype(F32)
        running[...] = jnp.zeros_like(running)
        gains[...] = jnp.ones_like(gains)

    proj = proj_ref[...]
    tile = proj[:, 0:512].astype(F32)
    ext[8 : 8 + BLOCK, :] = tile
    positions = first + lax.broadcasted_iota(jnp.int32, (BLOCK, 128), 0)
    start = doc_start(starts, positions)
    depth = jnp.concatenate([positions - start] * 4, axis=1)
    summed = taps_ref[3:4, :] * tile
    for lag in (1, 2, 3):
        window = ext[8 - lag : 8 - lag + BLOCK, :]
        summed = summed + jnp.where(depth >= lag, taps_ref[3 - lag : 4 - lag, :] * window, 0.0)
    act = jax.nn.silu(summed).astype(BF16)
    act_ref[...] = act
    ext[0:8, :] = tile[BLOCK - 8 :, :]

    step = jax.nn.softplus(proj[:, 512:640].astype(F32) + small_ref[0:1, :])
    decay = -jnp.exp(small_ref[1:2, :]) * step
    tri = (
        lax.broadcasted_iota(jnp.int32, (BLOCK, BLOCK), 1)
        <= lax.broadcasted_iota(jnp.int32, (BLOCK, BLOCK), 0)
    ).astype(F32)
    cumulative = jnp.dot(
        tri, decay, preferred_element_type=F32, precision=lax.Precision.HIGHEST
    )
    cum_ref[...] = cumulative
    step_ref[...] = step
    ending = cumulative[BLOCK - 1 : BLOCK, :]
    last_start = start[BLOCK - 1 : BLOCK, :]
    trailing = jnp.where(positions >= last_start, jnp.exp(ending - cumulative) * step, 0.0)
    weighted = (spread(trailing) * act[:, 0:256].astype(F32)).astype(BF16)
    local_state = lax.dot_general(
        act[:, 256:384], weighted, (((0,), (0,)), ((), ())), preferred_element_type=F32
    )
    factor = jnp.where(last_start < first, jnp.exp(ending), 0.0)
    factor = spread(jnp.broadcast_to(factor, (8, 128)))
    inside_ref[0] = running[...]
    gain_ref[0] = gains[...]
    running[...] = factor[0:1, :] * running[...] + local_state
    gains[...] = gains[...] * factor

    @pl.when(block == pl.num_programs(0) - 1)
    def _():
        packed_ref[0:STATE, :] = running[...].astype(BF16)
        high = gains[...].astype(BF16)
        low = (gains[...] - high.astype(F32)).astype(BF16)
        packed_ref[STATE : STATE + 16, :] = jnp.concatenate([high, low], axis=0)


def block_kernel(
    starts, base, act_ref, cum_ref, step_ref, inside_ref, gain_ref, y_ref, reach_ref
):
    first = base[0] + pl.program_id(0) * BLOCK
    act = act_ref[...]
    x_act, b_act, c_act = act[:, 0:256], act[:, 256:384], act[:, 384:512]
    cumulative = cum_ref[...]
    cum_rows, step_rows = cumulative.T, step_ref[...].T
    products = lax.dot_general(
        c_act, b_act, (((1,), (1,)), ((), ())), preferred_element_type=F32
    )
    start = doc_start(starts, first + lax.broadcasted_iota(jnp.int32, (BLOCK, 128), 0))
    row = lax.broadcasted_iota(jnp.int32, (BLOCK, BLOCK), 0)
    column = lax.broadcasted_iota(jnp.int32, (BLOCK, BLOCK), 1)
    allowed = (column <= row) & (first + column >= jnp.concatenate([start] * 2, axis=1))
    parts = []
    for h in range(4):
        gap = cumulative[:, h : h + 1] - cum_rows[h : h + 1, :]
        decay = jnp.exp(jnp.where(allowed, gap, FAR))
        scores = (products * decay * step_rows[h : h + 1, :]).astype(BF16)
        parts.append(
            jnp.dot(scores, x_act[:, h * WIDTH : (h + 1) * WIDTH], preferred_element_type=F32)
        )
    y_inner = jnp.concatenate(parts, axis=1)
    reach = spread(jnp.where(start < first, jnp.exp(cumulative), 0.0))
    inside = inside_ref[0]
    high = inside.astype(BF16)
    low = (inside - high.astype(F32)).astype(BF16)
    carried = jnp.dot(c_act, high, preferred_element_type=F32) + jnp.dot(
        c_act, low, preferred_element_type=F32
    )
    y_ref[...] = y_inner + reach * carried + x_act.astype(F32)
    reach_ref[...] = reach * gain_ref[0, 0:1, :]


def gain_of(packed):
    return packed[STATE : STATE + 8].astype(F32) + packed[STATE + 8 : STATE + 16].astype(F32)


def pair_kernel(scalars, own_ref, other_ref, eight_ref, nine_ref, out_ref):
    own, other = own_ref[...], other_ref[...]
    is_odd = scalars[0] % 2 == 1
    even, odd = jnp.where(is_odd, other, own), jnp.where(is_odd, own, other)
    before = eight_ref[0:STATE, :].astype(F32) + nine_ref[0:STATE, :].astype(F32)
    total = even[0:STATE].astype(F32) + gain_of(even)[0:1] * before
    total = odd[0:STATE].astype(F32) + gain_of(odd)[0:1] * total
    gain = gain_of(even) * gain_of(odd)
    high = gain.astype(BF16)
    low = (gain - high.astype(F32)).astype(BF16)
    out_ref[0:STATE, :] = total.astype(BF16)
    out_ref[STATE : STATE + 16, :] = jnp.concatenate([high, low], axis=0)


def finish_kernel(
    scalars, eight_ref, nine_ref, other_ref, pairs_ref, act_ref, y_ref, reach_ref, tok_ref, w_ref,
    out_ref, entering, weights,
):
    @pl.when(pl.program_id(0) == 0)
    def _():
        pair, odd = scalars[0] // 2, scalars[0] % 2
        state = eight_ref[0:STATE, :].astype(F32) + nine_ref[0:STATE, :].astype(F32)
        for k in range(PAIRS - 1):
            piece = pairs_ref[k]
            later = gain_of(piece)[0:1] * state + piece[0:STATE].astype(F32)
            state = jnp.where(k < pair, later, state)
        even = other_ref[...]
        later = gain_of(even)[0:1] * state + even[0:STATE].astype(F32)
        entering[...] = jnp.where(odd == 1, later, state).astype(BF16)
        for k in range(Z):
            for yh in range(YH):
                weights[pl.ds((yh * Z + k) * 256, 256), :] = w_ref[k, yh]

    gate = jnp.dot(tok_ref[...], weights[...], preferred_element_type=F32).astype(BF16)
    carried = jnp.dot(act_ref[...], entering[...], preferred_element_type=F32)
    total = y_ref[...] + reach_ref[...] * carried
    out_ref[...] = (total * jax.nn.silu(gate.astype(F32))).astype(BF16)


def shape(dims, dtype):
    return jax.ShapeDtypeStruct(dims, dtype)


def work(flops, moved, exps=0):
    return pl.CostEstimate(flops=flops, bytes_accessed=moved, transcendentals=exps)


def run_first(gathered, pieces, swapped, scalars):
    rows, depth = gathered.shape
    layout = tuple((offset, first, piece.shape[0]) for offset, first, piece in pieces)
    arrays = [in_hbm(piece) for _, _, piece in pieces] + [in_hbm(swapped)]
    last = rows // BLOCK - 1
    return call(
        functools.partial(first_kernel, layout),
        (1,),
        [pl.BlockSpec((BLOCK, depth), lambda *_: (last, 0))] + [whole(a.shape) for a in arrays],
        [pl.BlockSpec((BLOCK, 640), lambda *_: (last, 0)), held(None)],
        [shape((rows, 640), BF16), shape((depth, 640), BF16)],
        prefetch=1,
        cost=work(2 * BLOCK * depth * 640, 12 << 20),
        room=24,
    )(scalars, gathered, *arrays)


def run_rest(gathered, weights, proj):
    rows, depth = gathered.shape
    count = rows // BLOCK - 1
    return call(
        rest_kernel,
        (count,),
        [rows_of((BLOCK, depth)), held(weights), pl.BlockSpec(memory_space=pl.ANY)],
        rows_of((BLOCK, 640)),
        shape((rows, 640), BF16),
        cost=work(2 * count * BLOCK * depth * 640, 8 << 20),
        room=16,
        aliases={2: 0},
    )(gathered, weights, proj)


def run_state(starts, base, proj, rim, taps, small):
    rows = proj.shape[0]
    blocks = rows // BLOCK
    return call(
        state_kernel,
        (blocks,),
        [rows_of((BLOCK, 640)), whole((8, 512)), whole((4, 512)), whole((8, 128))],
        [
            rows_of((BLOCK, 512)),
            rows_of((BLOCK, 128)),
            rows_of((BLOCK, 128)),
            rows_of((1, STATE, 256)),
            rows_of((1, 8, 256)),
            whole((STATE + 16, 256)),
        ],
        [
            shape((rows, 512), BF16),
            shape((rows, 128), F32),
            shape((rows, 128), F32),
            shape((blocks, STATE, 256), F32),
            shape((blocks, 8, 256), F32),
            shape((STATE + 16, 256), BF16),
        ],
        scratch=[
            pltpu.VMEM((8 + BLOCK, 512), F32),
            pltpu.VMEM((STATE, 256), F32),
            pltpu.VMEM((8, 256), F32),
        ],
        prefetch=2,
        cost=work(2 * rows * 128 * 256, 4 << 20, rows * 1024),
    )(starts, base, proj, rim, taps, small)


def run_blocks(starts, base, act, cum, step, inside, gains):
    rows = act.shape[0]
    blocks = rows // BLOCK
    return call(
        block_kernel,
        (blocks,),
        [
            rows_of((BLOCK, 512)),
            rows_of((BLOCK, 128)),
            rows_of((BLOCK, 128)),
            rows_of((1, STATE, 256)),
            rows_of((1, 8, 256)),
        ],
        [rows_of((BLOCK, 256)), rows_of((BLOCK, 256))],
        [pltpu.HBM((rows, 256), F32), pltpu.HBM((rows, 256), F32)],
        prefetch=2,
        cost=work(2 * rows * 256 * 1024, 5 << 20, rows * 1280),
    )(starts, base, act, cum, step, inside, gains)


def run_pair(scalars, own, other, eight, nine):
    return call(
        pair_kernel,
        (1,),
        [held(own)] * 4,
        held(own),
        shape(own.shape, BF16),
        prefetch=1,
        cost=work(1 << 17, 1 << 18),
        room=4,
    )(scalars, own, other, eight, nine)


def run_finish(scalars, eight, nine, other, pairs, act, y, reach, gathered, gate_all):
    rows, depth = gathered.shape
    return call(
        finish_kernel,
        (rows // TALL,),
        [
            held(eight),
            held(nine),
            held(other),
            held(pairs),
            pl.BlockSpec((TALL, 128), lambda i, *_: (i, 3)),
            rows_of((TALL, 256)),
            rows_of((TALL, 256)),
            rows_of((TALL, depth)),
            whole(gate_all.shape),
        ],
        rows_of((TALL, 256)),
        shape((rows, 256), BF16),
        scratch=[pltpu.VMEM((STATE, 256), BF16), pltpu.VMEM((depth, 256), BF16)],
        prefetch=1,
        cost=work(2 * rows * (128 + depth) * 256, 13 << 20),
        room=28,
    )(scalars, eight, nine, other, pairs, act, y, reach, gathered, gate_all)


def local(
    tokens,
    doc_lengths,
    value_weight,
    gate_weight,
    state_weight,
    step_weight,
    value_conv,
    state_conv,
    step_bias,
    log_rate,
):
    tok_dev = tokens.shape[0] * X * Y * C
    heads_here = step_weight.shape[1]
    core = lax.axis_index("c")
    z = lax.axis_index(RING)
    group = lax.axis_index("x") * 2 + lax.axis_index("y") // 2
    gathered = lax.all_gather(tokens, HEAD, axis=0, tiled=True)

    state_half = lax.dynamic_slice(state_weight, (group, core * 128, 0), (1, 128, 256))[0]
    conv_own = lax.dynamic_index_in_dim(state_conv, group, 0, keepdims=False)
    step_rows = jnp.pad(step_weight.T, ((0, 8 - heads_here), (0, 0)))
    pack = jnp.concatenate([value_weight, state_half, step_rows, gate_weight], axis=0)
    both = lax.all_gather(pack, "yh", axis=0, tiled=False)
    pieces = ring_gather(both[:, :392])
    halves = jnp.concatenate([piece[:, 256:384] for _, _, piece in pieces], axis=0)
    halves = lax.ppermute(halves, "c", [(0, 1), (1, 0)])
    scalars = jnp.stack([z, core]).astype(jnp.int32)
    gate_part, gathered, halves = lax.optimization_barrier((both[:, 392:], gathered, halves))
    gate_all = lax.all_gather(gate_part, RING, axis=0, tiled=False)
    gathered = in_hbm(gathered)
    proj, weights = run_first(gathered, pieces, halves, scalars)
    rim = along_seq(proj[-8:, :512], 1)
    proj = run_rest(gathered, weights, proj)

    starts = (jnp.cumsum(doc_lengths) - doc_lengths).astype(jnp.int32)
    base = (lax.axis_index(SEQ) * tok_dev).astype(jnp.int32).reshape(1)
    taps = jnp.concatenate([value_conv, conv_own], axis=1)
    small = jnp.pad(jnp.stack([step_bias, log_rate]), ((0, 6), (0, 128 - heads_here)))
    act, cum, step, inside, gains, packed = run_state(starts, base, proj, rim, taps, small)
    eight = lax.ppermute(packed, SEQ, [(Z - 1, Z)])
    nine = lax.ppermute(packed, SEQ, [(Z - 1, Z + 1)])
    other = lax.ppermute(packed, "zc", ring(2, 1))
    y, reach = run_blocks(starts, base, act, cum, step, inside, gains)
    packed, other, eight, nine, y, reach = lax.optimization_barrier(
        (packed, other, eight, nine, y, reach)
    )
    pair = run_pair(scalars, packed, other, eight, nine)
    pairs = lax.all_gather(pair, "zh", axis=0, tiled=False)
    return run_finish(
        scalars, eight, nine, other, pairs, act, in_hbm(y), in_hbm(reach), gathered, in_hbm(gate_all)
    )


def solution(mesh):
    grid = Mesh(mesh.devices.reshape(YH, PAIRS, 2, X, Y, C), SEQ + HEAD)
    return jax.shard_map(
        local,
        mesh=grid,
        in_specs=(
            P(SEQ + HEAD, None),
            P(),
            P(SEQ, HEAD),
            P(SEQ, HEAD),
            P(None, SEQ, None),
            P(SEQ, HEAD),
            P(None, HEAD),
            P(),
            P(HEAD),
            P(HEAD),
        ),
        out_specs=P(SEQ, HEAD),
        check_vma=False,
    )
```

```python
import functools

import jax
import jax.numpy as jnp
from jax import lax
from jax.experimental import pallas as pl
from jax.experimental.pallas import tpu as pltpu
from jax.sharding import Mesh
from jax.sharding import PartitionSpec as P

HEADS = 128
GROUPS = 8
BLOCK = 256
STATE = 128
WIDTH = 64
YH, Z, X, Y, C = 2, 8, 4, 4, 2
PAIRS = Z // 2
RING = ("zh", "zc")
SEQ = ("yh",) + RING
HEAD = ("x", "y", "c")
F32 = jnp.float32
BF16 = jnp.bfloat16
MIB = 1024 * 1024
FAR = -1e30
TALL = 512


def ring(count, step):
    return [(i, (i + step) % count) for i in range(count)]


def along_seq(value, step):
    return lax.ppermute(value, SEQ, [(i, i + step) for i in range(YH * Z - step)])


def ring_gather(block):
    pieces = [(0, 0, block)]
    right = left = block
    for step in range(1, 4):
        right = lax.ppermute(right, RING, ring(Z, 1))
        left = lax.ppermute(left, RING, ring(Z, -1))
        pieces += [(Z - step, 0, right), (step, 0, left)]
    right = lax.ppermute(right[:1], RING, ring(Z, 1))
    left = lax.ppermute(left[1:], RING, ring(Z, -1))
    return pieces + [(4, 0, right), (4, 1, left)]


def call(
    kernel, grid, in_specs, out_specs, out_shape, scratch=(), prefetch=0, cost=None, room=12,
    aliases=None,
):
    return pl.pallas_call(
        kernel,
        grid_spec=pltpu.PrefetchScalarGridSpec(
            num_scalar_prefetch=prefetch,
            grid=grid,
            in_specs=in_specs,
            out_specs=out_specs,
            scratch_shapes=scratch,
        ),
        out_shape=out_shape,
        input_output_aliases=aliases or {},
        compiler_params=pltpu.CompilerParams(
            vmem_limit_bytes=room * MIB, dimension_semantics=("arbitrary",) * len(grid)
        ),
        cost_estimate=cost,
    )


def whole(shape):
    return pl.BlockSpec(shape, lambda *_: (0,) * len(shape))


def in_hbm(value):
    return pltpu.with_memory_space_constraint(value, pltpu.HBM)


def held(_):
    return pl.BlockSpec(memory_space=pltpu.VMEM)


def rows_of(shape):
    return pl.BlockSpec(shape, lambda i, *_: (i,) + (0,) * (len(shape) - 1))


def first_kernel(layout, scalars, tok_ref, *refs):
    pieces, other, proj_ref, out = refs[:-3], refs[-3], refs[-2], refs[-1]
    z, core = scalars[0], scalars[1]
    count = 0
    for (offset, first, yh_count), piece in zip(layout, pieces):
        source = lax.rem(z + offset, Z)
        for local_yh in range(yh_count):
            start = pl.multiple_of(((first + local_yh) * Z + source) * 256, 256)
            out[pl.ds(start, 256), 0:256] = piece[local_yh, 0:256, :]
            own = pl.multiple_of(start + core * 128, 128)
            its = pl.multiple_of(start + (1 - core) * 128, 128)
            out[pl.ds(own, 128), 256:512] = piece[local_yh, 256:384, :]
            out[pl.ds(its, 128), 256:512] = other[count, :, :]
            count += 1
            steps = piece[local_yh, 384:392, :].astype(F32).T
            steps = jnp.concatenate([steps, jnp.zeros((256, 120), F32)], axis=1)
            out[pl.ds(start, 256), 512:640] = steps.astype(BF16)
    project(tok_ref, out, proj_ref)


def project(tok_ref, w_ref, out_ref):
    out_ref[...] = jnp.dot(
        tok_ref[...], w_ref[...], preferred_element_type=F32
    ).astype(BF16)


def rest_kernel(tok_ref, w_ref, _, out_ref):
    project(tok_ref, w_ref, out_ref)


def spread(columns):
    rows = columns.shape[0]
    lane = lax.broadcasted_iota(jnp.int32, (rows, 128), 1)
    wide = [jnp.broadcast_to(columns[:, h : h + 1], (rows, 128)) for h in range(4)]
    return jnp.concatenate(
        [jnp.where(lane < WIDTH, wide[0], wide[1]), jnp.where(lane < WIDTH, wide[2], wide[3])],
        axis=1,
    )


def doc_start(starts, positions):
    found = jnp.zeros(positions.shape, jnp.int32)
    for j in range(16):
        found = jnp.where(starts[j] <= positions, starts[j], found)
    return found


def state_kernel(
    starts, base, proj_ref, rim_ref, taps_ref, small_ref,
    act_ref, cum_ref, step_ref, inside_ref, gain_ref, packed_ref,
    ext, running, gains,
):
    block = pl.program_id(0)
    first = base[0] + block * BLOCK

    @pl.when(block == 0)
    def _():
        ext[0:8, :] = rim_ref[...].astype(F32)
        running[...] = jnp.zeros_like(running)
        gains[...] = jnp.ones_like(gains)

    proj = proj_ref[...]
    tile = proj[:, 0:512].astype(F32)
    ext[8 : 8 + BLOCK, :] = tile
    positions = first + lax.broadcasted_iota(jnp.int32, (BLOCK, 128), 0)
    start = doc_start(starts, positions)
    depth = (positions - start)[:, 0:1]
    summed = taps_ref[3:4, :] * tile
    for lag in (1, 2, 3):
        window = ext[8 - lag : 8 - lag + BLOCK, :]
        summed = summed + jnp.where(depth >= lag, taps_ref[3 - lag : 4 - lag, :] * window, 0.0)
    act = jax.nn.silu(summed).astype(BF16)
    act_ref[...] = act
    ext[0:8, :] = tile[BLOCK - 8 :, :]

    step = jax.nn.softplus(proj[:, 512:640].astype(F32) + small_ref[0:1, :])
    decay = -jnp.exp(small_ref[1:2, :]) * step
    tri = (
        lax.broadcasted_iota(jnp.int32, (BLOCK, BLOCK), 1)
        <= lax.broadcasted_iota(jnp.int32, (BLOCK, BLOCK), 0)
    ).astype(F32)
    cumulative = jnp.dot(
        tri, decay, preferred_element_type=F32, precision=lax.Precision.HIGHEST
    )
    cum_ref[...] = cumulative
    step_ref[...] = step
    ending = cumulative[BLOCK - 1 : BLOCK, :]
    last_start = start[BLOCK - 1 : BLOCK, :]
    trailing = jnp.where(positions >= last_start, jnp.exp(ending - cumulative) * step, 0.0)
    weighted = (spread(trailing) * act[:, 0:256].astype(F32)).astype(BF16)
    local_state = lax.dot_general(
        act[:, 256:384], weighted, (((0,), (0,)), ((), ())), preferred_element_type=F32
    )
    factor = jnp.where(last_start < first, jnp.exp(ending), 0.0)
    factor = spread(jnp.broadcast_to(factor, (8, 128)))
    inside_ref[0] = running[...]
    gain_ref[0] = gains[...]
    running[...] = factor[0:1, :] * running[...] + local_state
    gains[...] = gains[...] * factor

    @pl.when(block == pl.num_programs(0) - 1)
    def _():
        packed_ref[0:STATE, :] = running[...].astype(BF16)
        high = gains[...].astype(BF16)
        low = (gains[...] - high.astype(F32)).astype(BF16)
        packed_ref[STATE : STATE + 16, :] = jnp.concatenate([high, low], axis=0)


def block_kernel(
    starts, base, act_ref, cum_ref, step_ref, inside_ref, gain_ref, y_ref, reach_ref
):
    first = base[0] + pl.program_id(0) * BLOCK
    act = act_ref[...]
    x_act, b_act, c_act = act[:, 0:256], act[:, 256:384], act[:, 384:512]
    cumulative = cum_ref[...]
    cum_rows, step_rows = cumulative.T, step_ref[...].T
    products = lax.dot_general(
        c_act, b_act, (((1,), (1,)), ((), ())), preferred_element_type=F32
    )
    start = doc_start(starts, first + lax.broadcasted_iota(jnp.int32, (BLOCK, 128), 0))
    row = lax.broadcasted_iota(jnp.int32, (BLOCK, BLOCK), 0)
    column = lax.broadcasted_iota(jnp.int32, (BLOCK, BLOCK), 1)
    allowed = (column <= row) & (first + column >= start[:, 0:1])
    parts = []
    for h in range(4):
        gap = cumulative[:, h : h + 1] - cum_rows[h : h + 1, :]
        decay = jnp.exp(jnp.where(allowed, gap, FAR))
        scores = (products * decay * step_rows[h : h + 1, :]).astype(BF16)
        parts.append(
            jnp.dot(scores, x_act[:, h * WIDTH : (h + 1) * WIDTH], preferred_element_type=F32)
        )
    y_inner = jnp.concatenate(parts, axis=1)
    reach = spread(jnp.where(start < first, jnp.exp(cumulative), 0.0))
    inside = inside_ref[0]
    high = inside.astype(BF16)
    low = (inside - high.astype(F32)).astype(BF16)
    carried = jnp.dot(c_act, high, preferred_element_type=F32) + jnp.dot(
        c_act, low, preferred_element_type=F32
    )
    y_ref[...] = y_inner + reach * carried + x_act.astype(F32)
    reach_ref[...] = reach * gain_ref[0, 0:1, :]


def gain_of(packed):
    return packed[STATE : STATE + 8].astype(F32) + packed[STATE + 8 : STATE + 16].astype(F32)


def pair_kernel(pair_ref, eight_ref, nine_ref, out_ref):
    even, odd = pair_ref[0], pair_ref[1]
    before = eight_ref[0:STATE, :].astype(F32) + nine_ref[0:STATE, :].astype(F32)
    total = even[0:STATE].astype(F32) + gain_of(even)[0:1] * before
    total = odd[0:STATE].astype(F32) + gain_of(odd)[0:1] * total
    gain = gain_of(even) * gain_of(odd)
    high = gain.astype(BF16)
    low = (gain - high.astype(F32)).astype(BF16)
    out_ref[0:STATE, :] = total.astype(BF16)
    out_ref[STATE : STATE + 16, :] = jnp.concatenate([high, low], axis=0)


def finish_kernel(
    scalars, eight_ref, nine_ref, own_ref, pairs_ref, act_ref, y_ref, reach_ref, tok_ref, w_ref,
    out_ref, entering, weights,
):
    @pl.when(pl.program_id(0) == 0)
    def _():
        pair, odd = scalars[0] // 2, scalars[0] % 2
        state = eight_ref[0:STATE, :].astype(F32) + nine_ref[0:STATE, :].astype(F32)
        for k in range(PAIRS - 1):
            piece = pairs_ref[k]
            later = gain_of(piece)[0:1] * state + piece[0:STATE].astype(F32)
            state = jnp.where(k < pair, later, state)
        even = own_ref[0]
        later = gain_of(even)[0:1] * state + even[0:STATE].astype(F32)
        entering[...] = jnp.where(odd == 1, later, state).astype(BF16)
        for k in range(Z):
            for slot in range(YH):
                row = ((scalars[2] + slot) % YH * Z + k) * 256
                weights[pl.ds(pl.multiple_of(row, 256), 256), :] = w_ref[k, slot]

    gate = jnp.dot(tok_ref[...], weights[...], preferred_element_type=F32).astype(BF16)
    carried = jnp.dot(act_ref[...], entering[...], preferred_element_type=F32)
    total = y_ref[...] + reach_ref[...] * carried
    out_ref[...] = (total * jax.nn.silu(gate.astype(F32))).astype(BF16)


def shape(dims, dtype):
    return jax.ShapeDtypeStruct(dims, dtype)


def work(flops, moved, exps=0):
    return pl.CostEstimate(flops=flops, bytes_accessed=moved, transcendentals=exps)


def run_first(gathered, pieces, swapped, scalars):
    rows, depth = gathered.shape
    layout = tuple((offset, first, piece.shape[0]) for offset, first, piece in pieces)
    arrays = [in_hbm(piece) for _, _, piece in pieces] + [in_hbm(swapped)]
    last = rows // BLOCK - 1
    return call(
        functools.partial(first_kernel, layout),
        (1,),
        [pl.BlockSpec((BLOCK, depth), lambda *_: (last, 0))] + [whole(a.shape) for a in arrays],
        [pl.BlockSpec((BLOCK, 640), lambda *_: (last, 0)), held(None)],
        [shape((rows, 640), BF16), shape((depth, 640), BF16)],
        prefetch=1,
        cost=work(2 * BLOCK * depth * 640, 12 << 20),
        room=24,
    )(scalars, gathered, *arrays)


def run_rest(gathered, weights, proj):
    rows, depth = gathered.shape
    count = rows // BLOCK - 1
    return call(
        rest_kernel,
        (count,),
        [rows_of((BLOCK, depth)), held(weights), pl.BlockSpec(memory_space=pl.ANY)],
        rows_of((BLOCK, 640)),
        shape((rows, 640), BF16),
        cost=work(2 * count * BLOCK * depth * 640, 8 << 20),
        room=16,
        aliases={2: 0},
    )(gathered, weights, proj)


def run_state(starts, base, proj, rim, taps, small):
    rows = proj.shape[0]
    blocks = rows // BLOCK
    return call(
        state_kernel,
        (blocks,),
        [rows_of((BLOCK, 640)), whole((8, 512)), whole((4, 512)), whole((8, 128))],
        [
            rows_of((BLOCK, 512)),
            rows_of((BLOCK, 128)),
            rows_of((BLOCK, 128)),
            rows_of((1, STATE, 256)),
            rows_of((1, 8, 256)),
            whole((STATE + 16, 256)),
        ],
        [
            shape((rows, 512), BF16),
            shape((rows, 128), F32),
            shape((rows, 128), F32),
            shape((blocks, STATE, 256), F32),
            shape((blocks, 8, 256), F32),
            shape((STATE + 16, 256), BF16),
        ],
        scratch=[
            pltpu.VMEM((8 + BLOCK, 512), F32),
            pltpu.VMEM((STATE, 256), F32),
            pltpu.VMEM((8, 256), F32),
        ],
        prefetch=2,
        cost=work(2 * rows * 128 * 256, 4 << 20, rows * 1024),
    )(starts, base, proj, rim, taps, small)


def run_blocks(starts, base, act, cum, step, inside, gains):
    rows = act.shape[0]
    blocks = rows // BLOCK
    return call(
        block_kernel,
        (blocks,),
        [
            rows_of((BLOCK, 512)),
            rows_of((BLOCK, 128)),
            rows_of((BLOCK, 128)),
            rows_of((1, STATE, 256)),
            rows_of((1, 8, 256)),
        ],
        [rows_of((BLOCK, 256)), rows_of((BLOCK, 256))],
        [pltpu.HBM((rows, 256), F32), pltpu.HBM((rows, 256), F32)],
        prefetch=2,
        cost=work(2 * rows * 256 * 1024, 5 << 20, rows * 1280),
    )(starts, base, act, cum, step, inside, gains)


def run_pair(pair, eight, nine):
    return call(
        pair_kernel,
        (1,),
        [held(pair), held(eight), held(nine)],
        held(eight),
        shape(eight.shape, BF16),
        cost=work(1 << 17, 1 << 18),
        room=4,
    )(pair, eight, nine)


def run_finish(scalars, eight, nine, own, pairs, act, y, reach, gathered, gate_all):
    rows, depth = gathered.shape
    return call(
        finish_kernel,
        (rows // TALL,),
        [
            held(eight),
            held(nine),
            held(own),
            held(pairs),
            pl.BlockSpec((TALL, 128), lambda i, *_: (i, 3)),
            rows_of((TALL, 256)),
            rows_of((TALL, 256)),
            rows_of((TALL, depth)),
            whole(gate_all.shape),
        ],
        rows_of((TALL, 256)),
        shape((rows, 256), BF16),
        scratch=[pltpu.VMEM((STATE, 256), BF16), pltpu.VMEM((depth, 256), BF16)],
        prefetch=1,
        cost=work(2 * rows * (128 + depth) * 256, 13 << 20),
        room=28,
    )(scalars, eight, nine, own, pairs, act, y, reach, gathered, gate_all)


def local(
    tokens,
    doc_lengths,
    value_weight,
    gate_weight,
    state_weight,
    step_weight,
    value_conv,
    state_conv,
    step_bias,
    log_rate,
):
    tok_dev = tokens.shape[0] * X * Y * C
    heads_here = step_weight.shape[1]
    core = lax.axis_index("c")
    z = lax.axis_index(RING)
    group = lax.axis_index("x") * 2 + lax.axis_index("y") // 2
    gathered = lax.all_gather(tokens, HEAD, axis=0, tiled=True)

    state_half = lax.dynamic_slice(state_weight, (group, core * 128, 0), (1, 128, 256))[0]
    conv_own = lax.dynamic_index_in_dim(state_conv, group, 0, keepdims=False)
    step_rows = jnp.pad(step_weight.T, ((0, 8 - heads_here), (0, 0)))
    pack = jnp.concatenate([value_weight, state_half, step_rows], axis=0)
    both = lax.all_gather(pack, "yh", axis=0, tiled=False)
    pieces = ring_gather(both)
    halves = jnp.concatenate([piece[:, 256:384] for _, _, piece in pieces], axis=0)
    gate_own, _ = lax.optimization_barrier((gate_weight, halves))
    halves = lax.ppermute(halves, "c", [(0, 1), (1, 0)])
    gate_far = lax.ppermute(gate_own, "yh", ring(YH, 1))
    scalars = jnp.stack([z, core, lax.axis_index("yh")]).astype(jnp.int32)
    gathered = in_hbm(gathered)
    proj, weights = run_first(gathered, pieces, halves, scalars)
    gate_far, proj = lax.optimization_barrier((gate_far, proj))
    gate_all = lax.all_gather(jnp.stack([gate_weight, gate_far]), RING, axis=0, tiled=False)
    rim = along_seq(proj[-8:, :512], 1)
    proj = run_rest(gathered, weights, proj)

    starts = (jnp.cumsum(doc_lengths) - doc_lengths).astype(jnp.int32)
    base = (lax.axis_index(SEQ) * tok_dev).astype(jnp.int32).reshape(1)
    taps = jnp.concatenate([value_conv, conv_own], axis=1)
    small = jnp.pad(jnp.stack([step_bias, log_rate]), ((0, 6), (0, 128 - heads_here)))
    act, cum, step, inside, gains, packed = run_state(starts, base, proj, rim, taps, small)
    eight = lax.ppermute(packed, SEQ, [(Z - 1, Z)])
    nine = lax.ppermute(packed, SEQ, [(Z - 1, Z + 1)])
    y, reach = run_blocks(starts, base, act, cum, step, inside, gains)
    packed, y, reach = lax.optimization_barrier((packed, y, reach))
    own = lax.all_gather(packed, "zc", axis=0, tiled=False)
    own, eight, nine = lax.optimization_barrier((own, eight, nine))
    pairs = lax.all_gather(run_pair(own, eight, nine), "zh", axis=0, tiled=False)
    return run_finish(
        scalars, eight, nine, own, pairs, act, in_hbm(y), in_hbm(reach), gathered, in_hbm(gate_all)
    )


def solution(mesh):
    grid = Mesh(mesh.devices.reshape(YH, PAIRS, 2, X, Y, C), SEQ + HEAD)
    return jax.shard_map(
        local,
        mesh=grid,
        in_specs=(
            P(SEQ + HEAD, None),
            P(),
            P(SEQ, HEAD),
            P(SEQ, HEAD),
            P(None, SEQ, None),
            P(SEQ, HEAD),
            P(None, HEAD),
            P(),
            P(HEAD),
            P(HEAD),
        ),
        out_specs=P(SEQ, HEAD),
        check_vma=False,
    )
```

```python
import functools

import jax
import jax.numpy as jnp
from jax import lax
from jax.experimental import pallas as pl
from jax.experimental.pallas import tpu as pltpu
from jax.sharding import Mesh
from jax.sharding import PartitionSpec as P

HEADS = 128
GROUPS = 8
BLOCK = 256
STATE = 128
WIDTH = 64
YH, Z, X, Y, C = 2, 8, 4, 4, 2
PAIRS = Z // 2
RING = ("zh", "zc")
SEQ = ("yh",) + RING
HEAD = ("x", "y", "c")
F32 = jnp.float32
BF16 = jnp.bfloat16
MIB = 1024 * 1024
FAR = -1e30
TALL = 512


def ring(count, step):
    return [(i, (i + step) % count) for i in range(count)]


def along_seq(value, step):
    return lax.ppermute(value, SEQ, [(i, i + step) for i in range(YH * Z - step)])


def ring_gather(block):
    pieces = [(0, 0, block)]
    right = left = block
    for step in range(1, 4):
        right = lax.ppermute(right, RING, ring(Z, 1))
        left = lax.ppermute(left, RING, ring(Z, -1))
        pieces += [(Z - step, 0, right), (step, 0, left)]
    right = lax.ppermute(right[:1], RING, ring(Z, 1))
    left = lax.ppermute(left[1:], RING, ring(Z, -1))
    return pieces + [(4, 0, right), (4, 1, left)]


def call(
    kernel, grid, in_specs, out_specs, out_shape, scratch=(), prefetch=0, cost=None, room=12,
    aliases=None,
):
    return pl.pallas_call(
        kernel,
        grid_spec=pltpu.PrefetchScalarGridSpec(
            num_scalar_prefetch=prefetch,
            grid=grid,
            in_specs=in_specs,
            out_specs=out_specs,
            scratch_shapes=scratch,
        ),
        out_shape=out_shape,
        input_output_aliases=aliases or {},
        compiler_params=pltpu.CompilerParams(
            vmem_limit_bytes=room * MIB, dimension_semantics=("arbitrary",) * len(grid)
        ),
        cost_estimate=cost,
    )


def whole(shape):
    return pl.BlockSpec(shape, lambda *_: (0,) * len(shape))


def in_hbm(value):
    return pltpu.with_memory_space_constraint(value, pltpu.HBM)


def held(_):
    return pl.BlockSpec(memory_space=pltpu.VMEM)


def rows_of(shape):
    return pl.BlockSpec(shape, lambda i, *_: (i,) + (0,) * (len(shape) - 1))


def first_kernel(layout, scalars, tok_ref, *refs):
    pieces, (other, proj_ref, far_ref, out, sem) = refs[:-5], refs[-5:]
    z, core = scalars[0], scalars[1]
    count = 0
    for (offset, first, yh_count), piece in zip(layout, pieces):
        source = lax.rem(z + offset, Z)
        for local_yh in range(yh_count):
            start = pl.multiple_of(((first + local_yh) * Z + source) * 256, 256)
            out[pl.ds(start, 256), 0:256] = piece[local_yh, 0:256, :]
            own = pl.multiple_of(start + core * 128, 128)
            its = pl.multiple_of(start + (1 - core) * 128, 128)
            out[pl.ds(own, 128), 256:512] = piece[local_yh, 256:384, :]
            out[pl.ds(its, 128), 256:512] = other[count, :, :]
            count += 1
            steps = piece[local_yh, 384:392, :].astype(F32).T
            steps = jnp.concatenate([steps, jnp.zeros((256, 120), F32)], axis=1)
            out[pl.ds(start, 256), 512:640] = steps.astype(BF16)
    copy = pltpu.make_async_copy(out, far_ref, sem)
    copy.start()
    project(tok_ref, out, proj_ref)
    copy.wait()


def project(tok_ref, w_ref, out_ref):
    out_ref[...] = jnp.dot(
        tok_ref[...], w_ref[...], preferred_element_type=F32
    ).astype(BF16)


def rest_kernel(tok_ref, w_ref, _, out_ref):
    project(tok_ref, w_ref, out_ref)


def spread(columns):
    rows = columns.shape[0]
    lane = lax.broadcasted_iota(jnp.int32, (rows, 128), 1)
    wide = [jnp.broadcast_to(columns[:, h : h + 1], (rows, 128)) for h in range(4)]
    return jnp.concatenate(
        [jnp.where(lane < WIDTH, wide[0], wide[1]), jnp.where(lane < WIDTH, wide[2], wide[3])],
        axis=1,
    )


def doc_start(starts, positions):
    found = jnp.zeros(positions.shape, jnp.int32)
    for j in range(16):
        found = jnp.where(starts[j] <= positions, starts[j], found)
    return found


def state_kernel(
    starts, base, proj_ref, rim_ref, taps_ref, small_ref,
    act_ref, cum_ref, step_ref, inside_ref, gain_ref, packed_ref,
    ext, running, gains,
):
    block = pl.program_id(0)
    first = base[0] + block * BLOCK

    @pl.when(block == 0)
    def _():
        ext[0:8, :] = rim_ref[...].astype(F32)
        running[...] = jnp.zeros_like(running)
        gains[...] = jnp.ones_like(gains)

    proj = proj_ref[...]
    tile = proj[:, 0:512].astype(F32)
    ext[8 : 8 + BLOCK, :] = tile
    positions = first + lax.broadcasted_iota(jnp.int32, (BLOCK, 128), 0)
    start = doc_start(starts, positions)
    depth = (positions - start)[:, 0:1]
    summed = taps_ref[3:4, :] * tile
    for lag in (1, 2, 3):
        window = ext[8 - lag : 8 - lag + BLOCK, :]
        summed = summed + jnp.where(depth >= lag, taps_ref[3 - lag : 4 - lag, :] * window, 0.0)
    act = jax.nn.silu(summed).astype(BF16)
    act_ref[...] = act
    ext[0:8, :] = tile[BLOCK - 8 :, :]

    step = jax.nn.softplus(proj[:, 512:640].astype(F32) + small_ref[0:1, :])
    decay = -jnp.exp(small_ref[1:2, :]) * step
    tri = (
        lax.broadcasted_iota(jnp.int32, (BLOCK, BLOCK), 1)
        <= lax.broadcasted_iota(jnp.int32, (BLOCK, BLOCK), 0)
    ).astype(F32)
    cumulative = jnp.dot(
        tri, decay, preferred_element_type=F32, precision=lax.Precision.HIGHEST
    )
    cum_ref[...] = cumulative
    step_ref[...] = step
    ending = cumulative[BLOCK - 1 : BLOCK, :]
    last_start = start[BLOCK - 1 : BLOCK, :]
    trailing = jnp.where(positions >= last_start, jnp.exp(ending - cumulative) * step, 0.0)
    weighted = (spread(trailing) * act[:, 0:256].astype(F32)).astype(BF16)
    local_state = lax.dot_general(
        act[:, 256:384], weighted, (((0,), (0,)), ((), ())), preferred_element_type=F32
    )
    factor = jnp.where(last_start < first, jnp.exp(ending), 0.0)
    factor = spread(jnp.broadcast_to(factor, (8, 128)))
    inside_ref[0] = running[...]
    gain_ref[0] = gains[...]
    running[...] = factor[0:1, :] * running[...] + local_state
    gains[...] = gains[...] * factor

    @pl.when(block == pl.num_programs(0) - 1)
    def _():
        packed_ref[0:STATE, :] = running[...].astype(BF16)
        high = gains[...].astype(BF16)
        low = (gains[...] - high.astype(F32)).astype(BF16)
        packed_ref[STATE : STATE + 16, :] = jnp.concatenate([high, low], axis=0)


def block_kernel(
    starts, base, act_ref, cum_ref, step_ref, inside_ref, gain_ref, y_ref, reach_ref
):
    first = base[0] + pl.program_id(0) * BLOCK
    act = act_ref[...]
    x_act, b_act, c_act = act[:, 0:256], act[:, 256:384], act[:, 384:512]
    cumulative = cum_ref[...]
    cum_rows, step_rows = cumulative.T, step_ref[...].T
    products = lax.dot_general(
        c_act, b_act, (((1,), (1,)), ((), ())), preferred_element_type=F32
    )
    start = doc_start(starts, first + lax.broadcasted_iota(jnp.int32, (BLOCK, 128), 0))
    row = lax.broadcasted_iota(jnp.int32, (BLOCK, BLOCK), 0)
    column = lax.broadcasted_iota(jnp.int32, (BLOCK, BLOCK), 1)
    allowed = (column <= row) & (first + column >= start[:, 0:1])
    parts = []
    for h in range(4):
        gap = cumulative[:, h : h + 1] - cum_rows[h : h + 1, :]
        decay = jnp.exp(jnp.where(allowed, gap, FAR))
        scores = (products * decay * step_rows[h : h + 1, :]).astype(BF16)
        parts.append(
            jnp.dot(scores, x_act[:, h * WIDTH : (h + 1) * WIDTH], preferred_element_type=F32)
        )
    y_inner = jnp.concatenate(parts, axis=1)
    reach = spread(jnp.where(start < first, jnp.exp(cumulative), 0.0))
    inside = inside_ref[0]
    high = inside.astype(BF16)
    low = (inside - high.astype(F32)).astype(BF16)
    carried = jnp.dot(c_act, high, preferred_element_type=F32) + jnp.dot(
        c_act, low, preferred_element_type=F32
    )
    y_ref[...] = y_inner + reach * carried + x_act.astype(F32)
    reach_ref[...] = reach * gain_ref[0, 0:1, :]


def gain_of(packed):
    return packed[STATE : STATE + 8].astype(F32) + packed[STATE + 8 : STATE + 16].astype(F32)


def pair_kernel(pair_ref, eight_ref, nine_ref, out_ref):
    even, odd = pair_ref[0], pair_ref[1]
    before = eight_ref[0:STATE, :].astype(F32) + nine_ref[0:STATE, :].astype(F32)
    total = even[0:STATE].astype(F32) + gain_of(even)[0:1] * before
    total = odd[0:STATE].astype(F32) + gain_of(odd)[0:1] * total
    gain = gain_of(even) * gain_of(odd)
    high = gain.astype(BF16)
    low = (gain - high.astype(F32)).astype(BF16)
    out_ref[0:STATE, :] = total.astype(BF16)
    out_ref[STATE : STATE + 16, :] = jnp.concatenate([high, low], axis=0)


def finish_kernel(
    scalars, eight_ref, nine_ref, own_ref, pairs_ref, act_ref, y_ref, reach_ref, tok_ref, w_ref,
    out_ref, entering, weights,
):
    @pl.when(pl.program_id(0) == 0)
    def _():
        pair, odd = scalars[0] // 2, scalars[0] % 2
        state = eight_ref[0:STATE, :].astype(F32) + nine_ref[0:STATE, :].astype(F32)
        for k in range(PAIRS - 1):
            piece = pairs_ref[k]
            later = gain_of(piece)[0:1] * state + piece[0:STATE].astype(F32)
            state = jnp.where(k < pair, later, state)
        even = own_ref[0]
        later = gain_of(even)[0:1] * state + even[0:STATE].astype(F32)
        entering[...] = jnp.where(odd == 1, later, state).astype(BF16)
        for k in range(Z):
            for slot in range(YH):
                row = ((scalars[2] + slot) % YH * Z + k) * 256
                weights[pl.ds(pl.multiple_of(row, 256), 256), :] = w_ref[k, slot]

    gate = jnp.dot(tok_ref[...], weights[...], preferred_element_type=F32).astype(BF16)
    carried = jnp.dot(act_ref[...], entering[...], preferred_element_type=F32)
    total = y_ref[...] + reach_ref[...] * carried
    out_ref[...] = (total * jax.nn.silu(gate.astype(F32))).astype(BF16)


def shape(dims, dtype):
    return jax.ShapeDtypeStruct(dims, dtype)


def work(flops, moved, exps=0):
    return pl.CostEstimate(flops=flops, bytes_accessed=moved, transcendentals=exps)


def run_first(gathered, pieces, swapped, scalars):
    rows, depth = gathered.shape
    layout = tuple((offset, first, piece.shape[0]) for offset, first, piece in pieces)
    arrays = [in_hbm(piece) for _, _, piece in pieces] + [in_hbm(swapped)]
    last = rows // BLOCK - 1
    return call(
        functools.partial(first_kernel, layout),
        (1,),
        [pl.BlockSpec((BLOCK, depth), lambda *_: (last, 0))] + [whole(a.shape) for a in arrays],
        [pl.BlockSpec((BLOCK, 640), lambda *_: (last, 0)), pl.BlockSpec(memory_space=pltpu.HBM)],
        [shape((rows, 640), BF16), pltpu.HBM((depth, 640), BF16)],
        scratch=[pltpu.VMEM((depth, 640), BF16), pltpu.SemaphoreType.DMA],
        prefetch=1,
        cost=work(2 * BLOCK * depth * 640, 12 << 20),
        room=32,
    )(scalars, gathered, *arrays)


def run_rest(gathered, weights, proj):
    rows, depth = gathered.shape
    count = rows // BLOCK - 1
    return call(
        rest_kernel,
        (count,),
        [rows_of((BLOCK, depth)), pl.BlockSpec((depth, 640), lambda *_: (0, 0), pipeline_mode=pl.Buffered(1)), pl.BlockSpec(memory_space=pl.ANY)],
        rows_of((BLOCK, 640)),
        shape((rows, 640), BF16),
        cost=work(2 * count * BLOCK * depth * 640, 8 << 20),
        room=24,
        aliases={2: 0},
    )(gathered, in_hbm(weights), proj)


def run_state(starts, base, proj, rim, taps, small):
    rows = proj.shape[0]
    blocks = rows // BLOCK
    return call(
        state_kernel,
        (blocks,),
        [rows_of((BLOCK, 640)), whole((8, 512)), whole((4, 512)), whole((8, 128))],
        [
            rows_of((BLOCK, 512)),
            rows_of((BLOCK, 128)),
            rows_of((BLOCK, 128)),
            rows_of((1, STATE, 256)),
            rows_of((1, 8, 256)),
            whole((STATE + 16, 256)),
        ],
        [
            shape((rows, 512), BF16),
            shape((rows, 128), F32),
            shape((rows, 128), F32),
            shape((blocks, STATE, 256), F32),
            shape((blocks, 8, 256), F32),
            shape((STATE + 16, 256), BF16),
        ],
        scratch=[
            pltpu.VMEM((8 + BLOCK, 512), F32),
            pltpu.VMEM((STATE, 256), F32),
            pltpu.VMEM((8, 256), F32),
        ],
        prefetch=2,
        cost=work(2 * rows * 128 * 256, 4 << 20, rows * 1024),
    )(starts, base, proj, rim, taps, small)


def run_blocks(starts, base, act, cum, step, inside, gains):
    rows = act.shape[0]
    blocks = rows // BLOCK
    return call(
        block_kernel,
        (blocks,),
        [
            rows_of((BLOCK, 512)),
            rows_of((BLOCK, 128)),
            rows_of((BLOCK, 128)),
            rows_of((1, STATE, 256)),
            rows_of((1, 8, 256)),
        ],
        [rows_of((BLOCK, 256)), rows_of((BLOCK, 256))],
        [pltpu.HBM((rows, 256), F32), pltpu.HBM((rows, 256), F32)],
        prefetch=2,
        cost=work(2 * rows * 256 * 1024, 5 << 20, rows * 1280),
    )(starts, base, act, cum, step, inside, gains)


def run_pair(pair, eight, nine):
    return call(
        pair_kernel,
        (1,),
        [held(pair), held(eight), held(nine)],
        held(eight),
        shape(eight.shape, BF16),
        cost=work(1 << 17, 1 << 18),
        room=4,
    )(pair, eight, nine)


def run_finish(scalars, eight, nine, own, pairs, act, y, reach, gathered, gate_all):
    rows, depth = gathered.shape
    return call(
        finish_kernel,
        (rows // TALL,),
        [
            held(eight),
            held(nine),
            held(own),
            held(pairs),
            pl.BlockSpec((TALL, 128), lambda i, *_: (i, 3)),
            rows_of((TALL, 256)),
            rows_of((TALL, 256)),
            rows_of((TALL, depth)),
            whole(gate_all.shape),
        ],
        rows_of((TALL, 256)),
        shape((rows, 256), BF16),
        scratch=[pltpu.VMEM((STATE, 256), BF16), pltpu.VMEM((depth, 256), BF16)],
        prefetch=1,
        cost=work(2 * rows * (128 + depth) * 256, 13 << 20),
        room=28,
    )(scalars, eight, nine, own, pairs, act, y, reach, gathered, gate_all)


def local(
    tokens,
    doc_lengths,
    value_weight,
    gate_weight,
    state_weight,
    step_weight,
    value_conv,
    state_conv,
    step_bias,
    log_rate,
):
    tok_dev = tokens.shape[0] * X * Y * C
    heads_here = step_weight.shape[1]
    core = lax.axis_index("c")
    z = lax.axis_index(RING)
    group = lax.axis_index("x") * 2 + lax.axis_index("y") // 2
    gathered = lax.all_gather(tokens, HEAD, axis=0, tiled=True)

    state_half = lax.dynamic_slice(state_weight, (group, core * 128, 0), (1, 128, 256))[0]
    conv_own = lax.dynamic_index_in_dim(state_conv, group, 0, keepdims=False)
    step_rows = jnp.pad(step_weight.T, ((0, 8 - heads_here), (0, 0)))
    pack = jnp.concatenate([value_weight, state_half, step_rows], axis=0)
    both = lax.all_gather(pack, "yh", axis=0, tiled=False)
    pieces = ring_gather(both)
    halves = jnp.concatenate([piece[:, 256:384] for _, _, piece in pieces], axis=0)
    gate_own, _ = lax.optimization_barrier((gate_weight, halves))
    halves = lax.ppermute(halves, "c", [(0, 1), (1, 0)])
    gate_far = lax.ppermute(gate_own, "yh", ring(YH, 1))
    scalars = jnp.stack([z, core, lax.axis_index("yh")]).astype(jnp.int32)
    gathered = in_hbm(gathered)
    proj, weights = run_first(gathered, pieces, halves, scalars)
    gate_far, proj = lax.optimization_barrier((gate_far, proj))
    gate_all = lax.all_gather(jnp.stack([gate_weight, gate_far]), RING, axis=0, tiled=False)
    rim = along_seq(proj[-8:, :512], 1)
    proj = run_rest(gathered, weights, proj)

    starts = (jnp.cumsum(doc_lengths) - doc_lengths).astype(jnp.int32)
    base = (lax.axis_index(SEQ) * tok_dev).astype(jnp.int32).reshape(1)
    taps = jnp.concatenate([value_conv, conv_own], axis=1)
    small = jnp.pad(jnp.stack([step_bias, log_rate]), ((0, 6), (0, 128 - heads_here)))
    act, cum, step, inside, gains, packed = run_state(starts, base, proj, rim, taps, small)
    eight = lax.ppermute(packed, SEQ, [(Z - 1, Z)])
    nine = lax.ppermute(packed, SEQ, [(Z - 1, Z + 1)])
    y, reach = run_blocks(starts, base, act, cum, step, inside, gains)
    packed, y, reach = lax.optimization_barrier((packed, y, reach))
    own = lax.all_gather(packed, "zc", axis=0, tiled=False)
    own, eight, nine = lax.optimization_barrier((own, eight, nine))
    pairs = lax.all_gather(run_pair(own, eight, nine), "zh", axis=0, tiled=False)
    return run_finish(
        scalars, eight, nine, own, pairs, act, in_hbm(y), in_hbm(reach), gathered, in_hbm(gate_all)
    )


def solution(mesh):
    grid = Mesh(mesh.devices.reshape(YH, PAIRS, 2, X, Y, C), SEQ + HEAD)
    return jax.shard_map(
        local,
        mesh=grid,
        in_specs=(
            P(SEQ + HEAD, None),
            P(),
            P(SEQ, HEAD),
            P(SEQ, HEAD),
            P(None, SEQ, None),
            P(SEQ, HEAD),
            P(None, HEAD),
            P(),
            P(HEAD),
            P(HEAD),
        ),
        out_specs=P(SEQ, HEAD),
        check_vma=False,
    )
```
